512 devices in a mesh: ctx: 128 (over z_hi, x, y), fsdp: 4 (over z_lo, core).
Axes of the slice: x: 4, y: 8, z: 8 (z_hi: 4, z_lo: 2; z = z_hi * 2 + z_lo), core: 2. Of those that a mesh axis runs over, the one named last changes fastest.
Arguments:
- query_in: bfloat16 [4, 16384, 2048], P('fsdp', 'ctx'), may hold values from -6 to 6
- key_in: bfloat16 [4, 16384, 2048], P('fsdp', 'ctx'), may hold values from -6 to 6
- value_in: bfloat16 [4, 16384, 2048], P('fsdp', 'ctx'), may hold values from -6 to 6
- feature_taps: float32 [3, 3, 2048], replicated, may hold values from -3 to 3
- decay_rate: float32 [128, 16], replicated, as said below
- residues: float32 [128, 16], replicated, may hold values from -3 to 3
- skip_gain: float32 [2048], replicated, may hold values from 0.5 to 1.5
- out_weight: bfloat16 [2048, 2048], P('fsdp'), may hold values from -0.1875 to 0.1875
Outputs:
- block_out: bfloat16 [4, 16384, 2048], P('fsdp', 'ctx')
The draws below stay inside these ranges and needn't reach their ends.
Inputs may be any that keep to these rules, and one draw needn't show every extreme that they name: `decay_rate`: every rate is positive.
All inputs are finite; a program needn't handle non-finite values.
Results may differ from the reference program's by a relative error of at most 0.0062.
Values may be sent and summed in bfloat16 or wider, within the bound.
A program may use at most 128 MiB of HBM per device.

```python
import math
import jax
import jax.numpy as jnp
from jax import lax

C = 2048
DOUT = 2048
GROUP = 16
MODES = 16
FEAT = 3
GROUPS = 128
LEN = 16384
SEQS = 4


def draw_decay_rate(key, part):
    coin_key = jax.random.fold_in(key, 11)
    slow_key = jax.random.fold_in(key, 12)
    fast_key = jax.random.fold_in(key, 13)
    share = 0.5
    slow = jnp.exp(jax.random.uniform(slow_key, (GROUPS, MODES), jnp.float32, math.log(0.1), math.log(2.0))) / LEN
    fast = jnp.exp(jax.random.uniform(fast_key, (GROUPS, MODES), jnp.float32, math.log(1.0 / 50.0), math.log(1.0 / 30.0)))
    picked = jax.random.bernoulli(coin_key, share, (GROUPS, MODES))
    return jnp.where(picked, slow, fast).astype(jnp.float32)


def with_spikes(drawn, stream_key, source, target, parts, factor):
    def block_of(position):
        return (jnp.arange(drawn.shape[position]) // (drawn.shape[position] // parts)).reshape((-1,) + (1,) * (drawn.ndim - 1 - position))

    near = jax.random.permutation(stream_key, parts)[block_of(target)]
    far = (block_of(target) + parts // 2) % parts
    return jnp.where((block_of(source) == near) | (block_of(source) == far), factor * drawn, drawn)


def block_levels(own_key, shape, shards, smallest, largest):
    factor_of, own = 1.0, jax.random.fold_in(own_key, 6)
    for dim, shards_of in shards:
        steps = jnp.exp(jax.random.uniform(jax.random.fold_in(own, dim), (shards_of,), jnp.float32, smallest / len(shards), largest / len(shards)))
        factor_of = factor_of * jnp.repeat(steps, shape[dim] // shards_of).reshape([-1 if axis == dim else 1 for axis in range(len(shape))])
    return factor_of


def bell_draw(key, extent, width, most, cuts=(), dtype=jnp.bfloat16):
    array = jax.random.normal(key, extent, jnp.float32) * width
    if len(cuts) > 0:
        array = block_levels(key, extent, cuts, -0.22, 0.18) * array
    return jnp.clip(array, min=-most, max=most).astype(dtype)


def gaussian_with(rng, extent, deviation, reach, split, heavy, kind=jnp.bfloat16):
    array = deviation * jax.random.normal(rng, extent, jnp.float32)
    if split:
        array = array * block_levels(rng, extent, split, -0.22, 0.18)
    return jnp.clip(with_spikes(array, jax.random.fold_in(rng, 3), *heavy), -reach, reach).astype(kind)


def setup_inputs(seed: int = 0) -> dict:
    key_of = jax.random.split(jax.random.key(seed), 9)
    return {
        "query_in": bell_draw(key_of[0], (SEQS, LEN, C), 1.0, 6.0, ((0, 4), (1, 128))),
        "key_in": bell_draw(key_of[1], (SEQS, LEN, C), 1.0, 6.0, ((0, 4), (1, 128))),
        "value_in": bell_draw(key_of[2], (SEQS, LEN, C), 1.0, 6.0, ((0, 4), (1, 128))),
        "feature_taps": bell_draw(key_of[3], (3, FEAT, C), 0.5, 3.0, (), jnp.float32),
        "decay_rate": draw_decay_rate(jax.random.fold_in(key_of[8], 71), 0),
        "residues": bell_draw(key_of[5], (GROUPS, MODES), 0.5, 3.0, (), jnp.float32),
        "skip_gain": jnp.clip(jax.random.uniform(key_of[6], (C,), jnp.float32, 0.5, 1.5), 0.5, 1.5),
        "out_weight": gaussian_with(key_of[7], (C, DOUT), C ** -0.5, 0.1875, ((0, 4),), (0, 1, 4, 2.0)),
    }


def featurize(rows, taps_one):
    values = rows.astype(jnp.float32)
    total = taps_one[0] * values
    for offset in range(1, FEAT):
        moved = jnp.concatenate([jnp.zeros((offset, values.shape[1]), jnp.float32), values[:-offset]], axis=0)
        total = total + taps_one[offset] * moved
    return total

def group_filter(rate_row, residue_row, length):
    steps_axis = jnp.arange(length).astype(jnp.float32)
    scale = residue_row * jnp.sqrt(-jnp.expm1(-2.0 * rate_row))
    return lax.optimization_barrier(jnp.sum(scale[:, None] * jnp.exp(-rate_row[:, None] * steps_axis[None, :]), axis=0))

def group_conv(operands):
    rate_row, residue_row, signal = operands
    length = signal.shape[0]
    kernel = group_filter(rate_row, residue_row, length)
    spectrum = jnp.fft.rfft(kernel, 2 * length)
    signal_spec = jnp.fft.rfft(signal, 2 * length, axis=0)
    return jnp.fft.irfft(spectrum[:, None] * signal_spec, 2 * length, axis=0)[:length]

def one_sequence(query_rows, key_rows, value_rows, feature_taps, decay_rate, residues, skip_gain, out_weight):
    featured_q = featurize(query_rows, feature_taps[0])
    featured_k = featurize(key_rows, feature_taps[1])
    featured_v = featurize(value_rows, feature_taps[2])
    kv_round = lax.optimization_barrier((featured_k * featured_v).astype(jnp.bfloat16))
    kv_float = kv_round.astype(jnp.float32)
    length = kv_float.shape[0]
    grouped = jnp.transpose(kv_float.reshape(length, GROUPS, GROUP), (1, 0, 2))
    conv_groups = lax.map(group_conv, (decay_rate, residues, grouped))
    conv_rows = jnp.transpose(conv_groups, (1, 0, 2)).reshape(length, C)
    convolved = lax.optimization_barrier(conv_rows.astype(jnp.bfloat16))
    gated = (featured_q * (convolved.astype(jnp.float32) + skip_gain * kv_float)).astype(jnp.bfloat16)
    return jnp.dot(gated, out_weight, preferred_element_type=jnp.float32).astype(jnp.bfloat16)

def reference(query_in, key_in, value_in, feature_taps, decay_rate, residues, skip_gain, out_weight):
    results = []
    for number in range(SEQS):
        results.append(one_sequence(query_in[number], key_in[number], value_in[number], feature_taps, decay_rate, residues, skip_gain, out_weight))
    return jnp.stack(results)
```

```python
import jax
import jax.numpy as jnp
from jax import lax
from jax.sharding import PartitionSpec as P

GROUP = 16
FEAT = 3

exact_precision = lax.Precision.HIGHEST


def shifted(shard, axis, by):
    count = lax.axis_size(axis)
    pairs = [(i, i + by) for i in range(count) if 0 <= i + by < count]
    return lax.ppermute(shard, axis, pairs)


def featurize(rows, tail, taps_one):
    values = jnp.concatenate([tail, rows], axis=0).astype(jnp.float32)
    count = rows.shape[0]
    total = taps_one[0] * values[FEAT - 1 :]
    for offset in range(1, FEAT):
        total = total + taps_one[offset] * values[FEAT - 1 - offset : FEAT - 1 - offset + count]
    return total


def split_bf16(values):
    high = values.astype(jnp.bfloat16)
    low = (values - high.astype(jnp.float32)).astype(jnp.bfloat16)
    return high, low


def two_pass(spec, table, signal):
    high, low = split_bf16(table)
    first = jnp.einsum(spec, high, signal, preferred_element_type=jnp.float32)
    return first + jnp.einsum(spec, low, signal, preferred_element_type=jnp.float32)


def toeplitz(kernel):
    width = kernel.shape[1]
    lag = lax.optimization_barrier(jnp.arange(width, dtype=jnp.int32))
    diff = lag[:, None] - lag[None, :]
    onehot = (lag[:, None, None] == diff[None, :, :]).astype(jnp.bfloat16)
    high, low = split_bf16(kernel)
    first = jnp.einsum("gs,sij->gij", high, onehot, preferred_element_type=jnp.float32)
    return first + jnp.einsum("gs,sij->gij", low, onehot, preferred_element_type=jnp.float32)


def local(query_in, key_in, value_in, feature_taps, decay_rate, residues, skip_gain, out_weight):
    query_rows = query_in[0]
    key_rows = key_in[0]
    value_rows = value_in[0]
    rows_here, chans = query_rows.shape
    keep = FEAT - 1
    tails = shifted(
        jnp.concatenate(
            [query_rows[rows_here - keep :], key_rows[rows_here - keep :], value_rows[rows_here - keep :]],
            axis=0,
        ),
        "ctx",
        1,
    )
    featured_q = featurize(query_rows, tails[0:keep], feature_taps[0])
    featured_k = featurize(key_rows, tails[keep : 2 * keep], feature_taps[1])
    featured_v = featurize(value_rows, tails[2 * keep :], feature_taps[2])
    kv_round = (featured_k * featured_v).astype(jnp.bfloat16)

    groups = chans // GROUP
    width = rows_here
    kv_grouped = kv_round.reshape(width, groups, GROUP)

    positions = jnp.arange(width, dtype=jnp.float32)
    scale = residues * jnp.sqrt(-jnp.expm1(-2.0 * decay_rate))
    powers = jnp.exp(-decay_rate[:, :, None] * positions)
    kernel = jnp.einsum("gm,gmt->gt", scale, powers, precision=exact_precision)
    closing = jnp.exp(-decay_rate[:, :, None] * (width - 1.0 - positions))
    lagged = jnp.exp(-decay_rate[:, :, None] * (positions + 1.0)) * scale[:, :, None]

    inner = two_pass("gij,jgc->igc", toeplitz(kernel), kv_grouped)
    ending = two_pass("gnj,jgc->gnc", closing, kv_grouped)

    count = lax.axis_size("ctx")
    entering = shifted(ending, "ctx", 1)
    if count > 2:
        step_decay = jnp.exp(-decay_rate * float(width))[:, :, None]
        entering = entering + step_decay * shifted(ending, "ctx", 2)
        span = 2
        while span < count:
            decay = jnp.exp(-decay_rate * float(width * span))[:, :, None]
            entering = entering + decay * shifted(entering, "ctx", span)
            span *= 2
    crossing = jnp.einsum("gni,gnc->igc", lagged, entering, precision=exact_precision)
    convolved = (inner + crossing).reshape(width, chans).astype(jnp.bfloat16)

    gated = (
        featured_q * (convolved.astype(jnp.float32) + skip_gain * kv_round.astype(jnp.float32))
    ).astype(jnp.bfloat16)
    block_out = jnp.dot(
        gated,
        lax.all_gather(out_weight, "fsdp", axis=0, tiled=True),
        preferred_element_type=jnp.float32,
    ).astype(jnp.bfloat16)
    return block_out[None]


def solution(mesh):
    return jax.shard_map(
        local,
        mesh=mesh,
        in_specs=(
            P("fsdp", "ctx", None),
            P("fsdp", "ctx", None),
            P("fsdp", "ctx", None),
            P(),
            P(),
            P(),
            P(),
            P("fsdp", None),
        ),
        out_specs=P("fsdp", "ctx", None),
        check_vma=False,
    )
```

```python
import jax
import jax.numpy as jnp
from jax import lax
from jax.sharding import PartitionSpec as P

GROUP = 16
FEAT = 3

exact_precision = lax.Precision.HIGHEST


def shifted(shard, axis, by):
    count = lax.axis_size(axis)
    pairs = [(i, i + by) for i in range(count) if 0 <= i + by < count]
    return lax.ppermute(shard, axis, pairs)


def featurize(rows, tail, taps_one):
    values = jnp.concatenate([tail, rows], axis=0).astype(jnp.float32)
    count = rows.shape[0]
    total = taps_one[0] * values[FEAT - 1 :]
    for offset in range(1, FEAT):
        total = total + taps_one[offset] * values[FEAT - 1 - offset : FEAT - 1 - offset + count]
    return total


def split_bf16(values):
    rounded = lax.reduce_precision(values, exponent_bits=8, mantissa_bits=7)
    return rounded.astype(jnp.bfloat16), (values - rounded).astype(jnp.bfloat16)


def two_pass(spec, table, signal):
    high, low = split_bf16(table)
    first = jnp.einsum(spec, high, signal, preferred_element_type=jnp.float32)
    return first + jnp.einsum(spec, low, signal, preferred_element_type=jnp.float32)


def toeplitz(kernel):
    width = kernel.shape[1]
    lag = lax.optimization_barrier(jnp.arange(width, dtype=jnp.int32))
    diff = lag[:, None] - lag[None, :]
    onehot = (lag[:, None, None] == diff[None, :, :]).astype(jnp.bfloat16)
    high, low = split_bf16(kernel)
    first = jnp.einsum("gs,sij->gij", high, onehot, preferred_element_type=jnp.float32)
    return first + jnp.einsum("gs,sij->gij", low, onehot, preferred_element_type=jnp.float32)


def gather_weight(out_weight):
    pair = [(0, 1), (1, 0)]
    chip = lax.axis_index("zlo")
    core = lax.axis_index("core")
    cores = lax.axis_size("core")
    mine = chip * cores + core
    remote = lax.ppermute(out_weight, "zlo", pair)
    neighbour = lax.ppermute(out_weight, "core", pair)
    relayed = lax.ppermute(remote, "core", pair)
    other_chip = (1 - chip) * cores
    return [
        (mine, out_weight),
        (chip * cores + 1 - core, neighbour),
        (other_chip + core, remote),
        (other_chip + 1 - core, relayed),
    ]


def local(query_in, key_in, value_in, feature_taps, decay_rate, residues, skip_gain, out_weight):
    weight_blocks = gather_weight(out_weight)
    query_rows = query_in[0]
    key_rows = key_in[0]
    value_rows = value_in[0]
    rows_here, chans = query_rows.shape
    keep = FEAT - 1
    tails = shifted(
        jnp.concatenate(
            [query_rows[rows_here - keep :], key_rows[rows_here - keep :], value_rows[rows_here - keep :]],
            axis=0,
        ),
        "ctx",
        1,
    )
    featured_q = featurize(query_rows, tails[0:keep], feature_taps[0])
    featured_k = featurize(key_rows, tails[keep : 2 * keep], feature_taps[1])
    featured_v = featurize(value_rows, tails[2 * keep :], feature_taps[2])
    kv_round = (featured_k * featured_v).astype(jnp.bfloat16)

    groups = chans // GROUP
    width = rows_here
    kv_grouped = kv_round.reshape(width, groups, GROUP)

    positions = jnp.arange(width, dtype=jnp.float32)
    scale = residues * jnp.sqrt(-jnp.expm1(-2.0 * decay_rate))
    powers = jnp.exp(-decay_rate[:, :, None] * positions)
    kernel = jnp.einsum("gm,gmt->gt", scale, powers, precision=exact_precision)
    closing = jnp.exp(-decay_rate[:, :, None] * (width - 1.0 - positions))
    lagged = jnp.exp(-decay_rate[:, :, None] * (positions + 1.0)) * scale[:, :, None]

    inner = two_pass("gij,jgc->igc", toeplitz(kernel), kv_grouped)
    ending = two_pass("gnj,jgc->gnc", closing, kv_grouped)

    count = lax.axis_size("ctx")
    entering = shifted(ending, "ctx", 1)
    if count > 2:
        step_decay = jnp.exp(-decay_rate * float(width))[:, :, None]
        entering = entering + step_decay * shifted(ending, "ctx", 2)
        span = 2
        while span < count:
            decay = jnp.exp(-decay_rate * float(width * span))[:, :, None]
            entering = entering + decay * shifted(entering, "ctx", span)
            span *= 2
    crossing = jnp.einsum("gni,gnc->igc", lagged, entering, precision=exact_precision)
    convolved = (inner + crossing).reshape(width, chans).astype(jnp.bfloat16)

    gated = (
        featured_q * (convolved.astype(jnp.float32) + skip_gain * kv_round.astype(jnp.float32))
    ).astype(jnp.bfloat16)
    rows = out_weight.shape[0]
    block_out = None
    for owner, weight in weight_blocks:
        columns = lax.dynamic_slice_in_dim(gated, owner * rows, rows, axis=1)
        term = jnp.dot(columns, weight, preferred_element_type=jnp.float32)
        block_out = term if block_out is None else block_out + term
    return block_out.astype(jnp.bfloat16)[None]


def solution(mesh):
    ctx_size, fsdp_size = mesh.shape["ctx"], mesh.shape["fsdp"]
    split = jax.sharding.Mesh(
        mesh.devices.reshape(ctx_size, fsdp_size // 2, 2), ("ctx", "zlo", "core")
    )
    batch = ("zlo", "core")
    return jax.shard_map(
        local,
        mesh=split,
        in_specs=(
            P(batch, "ctx", None),
            P(batch, "ctx", None),
            P(batch, "ctx", None),
            P(),
            P(),
            P(),
            P(),
            P(batch, None),
        ),
        out_specs=P(batch, "ctx", None),
        check_vma=False,
    )
```

```python
import functools

import jax
import jax.numpy as jnp
from jax import lax
from jax.experimental import pallas as pl
from jax.experimental.pallas import tpu as pltpu
from jax.sharding import PartitionSpec as P

GROUP = 16
FEAT = 3

exact_precision = lax.Precision.HIGHEST


def shifted(shard, axis, by):
    count = lax.axis_size(axis)
    pairs = [(i, i + by) for i in range(count) if 0 <= i + by < count]
    return lax.ppermute(shard, axis, pairs)


def featurize(rows, tail, taps_one):
    values = jnp.concatenate([tail, rows], axis=0).astype(jnp.float32)
    count = rows.shape[0]
    total = taps_one[0] * values[FEAT - 1 :]
    for offset in range(1, FEAT):
        total = total + taps_one[offset] * values[FEAT - 1 - offset : FEAT - 1 - offset + count]
    return total


def split_bf16(values):
    rounded = lax.reduce_precision(values, exponent_bits=8, mantissa_bits=7)
    return rounded.astype(jnp.bfloat16), (values - rounded).astype(jnp.bfloat16)


def two_pass(spec, table, signal):
    high, low = split_bf16(table)
    first = jnp.einsum(spec, high, signal, preferred_element_type=jnp.float32)
    return first + jnp.einsum(spec, low, signal, preferred_element_type=jnp.float32)


def toeplitz(kernel):
    width = kernel.shape[1]
    lag = lax.optimization_barrier(jnp.arange(width, dtype=jnp.int32))
    diff = lag[:, None] - lag[None, :]
    onehot = (lag[:, None, None] == diff[None, :, :]).astype(jnp.bfloat16)
    high, low = split_bf16(kernel)
    first = jnp.einsum("gs,sij->gij", high, onehot, preferred_element_type=jnp.float32)
    return first + jnp.einsum("gs,sij->gij", low, onehot, preferred_element_type=jnp.float32)


def gather_weight(out_weight):
    pair = [(0, 1), (1, 0)]
    chip = lax.axis_index("zlo")
    core = lax.axis_index("core")
    cores = lax.axis_size("core")
    mine = chip * cores + core
    remote = lax.ppermute(out_weight, "zlo", pair)
    neighbour = lax.ppermute(out_weight, "core", pair)
    relayed = lax.ppermute(remote, "core", pair)
    other_chip = (1 - chip) * cores
    return [
        (mine, out_weight),
        (chip * cores + 1 - core, neighbour),
        (other_chip + core, remote),
        (other_chip + 1 - core, relayed),
    ]


def scan_shifts(count):
    first = [1, 2] if count > 2 else [1]
    later = []
    span = 2
    while span < count:
        later.append(span)
        span *= 2
    return first, later


def scan_kernel(count, ending_ref, decay_ref, entering_ref, sent, landed, send_sem, recv_sem):
    me = lax.axis_index("ctx")
    first, later = scan_shifts(count)
    partners = sorted(set(first + later))

    barrier = pltpu.get_barrier_semaphore()
    for span in partners:
        for target in (lax.rem(me + span, count), lax.rem(me + count - span, count)):
            pl.semaphore_signal(barrier, inc=1, device_id={"ctx": target}, device_id_type=pl.DeviceIdType.MESH)
    pl.semaphore_wait(barrier, 2 * len(partners))

    def send(source, slot, span):
        copy = pltpu.make_async_remote_copy(
            src_ref=source,
            dst_ref=landed.at[slot],
            send_sem=send_sem.at[slot],
            recv_sem=recv_sem.at[slot],
            device_id={"ctx": lax.rem(me + span, count)},
            device_id_type=pl.DeviceIdType.MESH,
        )
        copy.start()
        return copy

    def arrived(slot, span):
        return jnp.where(me >= span, landed[slot], 0.0)

    copies = [send(ending_ref, slot, span) for slot, span in enumerate(first)]
    for copy in copies:
        copy.wait_recv()
    total = arrived(0, first[0])
    if len(first) > 1:
        total = total + decay_ref[0] * arrived(1, first[1])
    for step, span in enumerate(later):
        slot = len(first) + step
        sent[step] = total
        copies.append(send(sent.at[step], slot, span))
        copies[-1].wait_recv()
        total = total + decay_ref[step + 1] * arrived(slot, span)
    entering_ref[...] = total
    for copy in copies:
        copy.wait_send()


def scan_states(ending, decay):
    count = lax.axis_size("ctx")
    first, later = scan_shifts(count)
    slots = len(first) + len(later)
    vmem = pl.BlockSpec(memory_space=pltpu.VMEM)
    return pl.pallas_call(
        functools.partial(scan_kernel, count),
        out_shape=jax.ShapeDtypeStruct(ending.shape, jnp.float32),
        in_specs=[vmem, vmem],
        out_specs=vmem,
        scratch_shapes=[
            pltpu.VMEM((max(1, len(later)),) + ending.shape, jnp.float32),
            pltpu.VMEM((slots,) + ending.shape, jnp.float32),
            pltpu.SemaphoreType.DMA((slots,)),
            pltpu.SemaphoreType.DMA((slots,)),
        ],
        compiler_params=pltpu.CompilerParams(collective_id=0, has_side_effects=True),
    )(ending, decay)


def local(query_in, key_in, value_in, feature_taps, decay_rate, residues, skip_gain, out_weight):
    weight_blocks = gather_weight(out_weight)
    query_rows = query_in[0]
    key_rows = key_in[0]
    value_rows = value_in[0]
    rows_here, chans = query_rows.shape
    keep = FEAT - 1
    tails = shifted(
        jnp.concatenate(
            [query_rows[rows_here - keep :], key_rows[rows_here - keep :], value_rows[rows_here - keep :]],
            axis=0,
        ),
        "ctx",
        1,
    )
    featured_q = featurize(query_rows, tails[0:keep], feature_taps[0])
    featured_k = featurize(key_rows, tails[keep : 2 * keep], feature_taps[1])
    featured_v = featurize(value_rows, tails[2 * keep :], feature_taps[2])
    kv_round = (featured_k * featured_v).astype(jnp.bfloat16)

    groups = chans // GROUP
    width = rows_here
    kv_grouped = kv_round.reshape(width, groups, GROUP)

    positions = jnp.arange(width, dtype=jnp.float32)
    scale = residues * jnp.sqrt(-jnp.expm1(-2.0 * decay_rate))
    powers = jnp.exp(-decay_rate[:, :, None] * positions)
    kernel = jnp.einsum("gm,gmt->gt", scale, powers, precision=exact_precision)
    closing = jnp.exp(-decay_rate[:, :, None] * (width - 1.0 - positions))
    lagged = jnp.exp(-decay_rate[:, :, None] * (positions + 1.0)) * scale[:, :, None]

    inner = two_pass("gij,jgc->igc", toeplitz(kernel), kv_grouped)
    ending = two_pass("gnj,jgc->ngc", closing, kv_grouped).reshape(-1, chans)

    first, later = scan_shifts(lax.axis_size("ctx"))
    spans = jnp.asarray([1] * (len(first) - 1) + later, jnp.float32)[:, None, None] * float(width)
    decay = jnp.exp(-jnp.transpose(decay_rate)[None, :, :] * spans)
    decay = jnp.repeat(decay, GROUP, axis=2)
    entering = scan_states(ending, decay).reshape(-1, groups, GROUP)
    crossing = jnp.einsum("gni,ngc->igc", lagged, entering, precision=exact_precision)
    convolved = (inner + crossing).reshape(width, chans).astype(jnp.bfloat16)

    gated = (
        featured_q * (convolved.astype(jnp.float32) + skip_gain * kv_round.astype(jnp.float32))
    ).astype(jnp.bfloat16)
    rows = out_weight.shape[0]
    block_out = None
    for owner, weight in weight_blocks:
        columns = lax.dynamic_slice_in_dim(gated, owner * rows, rows, axis=1)
        term = jnp.dot(columns, weight, preferred_element_type=jnp.float32)
        block_out = term if block_out is None else block_out + term
    return block_out.astype(jnp.bfloat16)[None]


def solution(mesh):
    ctx_size, fsdp_size = mesh.shape["ctx"], mesh.shape["fsdp"]
    split = jax.sharding.Mesh(
        mesh.devices.reshape(ctx_size, fsdp_size // 2, 2), ("ctx", "zlo", "core")
    )
    batch = ("zlo", "core")
    return jax.shard_map(
        local,
        mesh=split,
        in_specs=(
            P(batch, "ctx", None),
            P(batch, "ctx", None),
            P(batch, "ctx", None),
            P(),
            P(),
            P(),
            P(),
            P(batch, None),
        ),
        out_specs=P(batch, "ctx", None),
        check_vma=False,
    )
```

```python
import functools

import jax
import jax.numpy as jnp
from jax import lax
from jax.experimental import pallas as pl
from jax.experimental.pallas import tpu as pltpu
from jax.sharding import PartitionSpec as P

GROUP = 16
FEAT = 3

exact_precision = lax.Precision.HIGHEST


def shifted(shard, axis, by):
    count = lax.axis_size(axis)
    pairs = [(i, i + by) for i in range(count) if 0 <= i + by < count]
    return lax.ppermute(shard, axis, pairs)


def featurize(rows, tail, taps_one):
    values = jnp.concatenate([tail, rows], axis=0).astype(jnp.float32)
    count = rows.shape[0]
    total = taps_one[0] * values[FEAT - 1 :]
    for offset in range(1, FEAT):
        total = total + taps_one[offset] * values[FEAT - 1 - offset : FEAT - 1 - offset + count]
    return total


def split_bf16(values):
    rounded = lax.reduce_precision(values, exponent_bits=8, mantissa_bits=7)
    return rounded.astype(jnp.bfloat16), (values - rounded).astype(jnp.bfloat16)


def two_pass(spec, table, signal):
    high, low = split_bf16(table)
    first = jnp.einsum(spec, high, signal, preferred_element_type=jnp.float32)
    return first + jnp.einsum(spec, low, signal, preferred_element_type=jnp.float32)


def toeplitz(kernel):
    width = kernel.shape[1]
    lag = lax.optimization_barrier(jnp.arange(width, dtype=jnp.int32))
    diff = lag[:, None] - lag[None, :]
    onehot = (lag[:, None, None] == diff[None, :, :]).astype(jnp.bfloat16)
    return [
        jnp.einsum("gs,sij->gij", part, onehot, preferred_element_type=jnp.bfloat16)
        for part in split_bf16(kernel)
    ]


def gather_weight(out_weight):
    pair = [(0, 1), (1, 0)]
    chip = lax.axis_index("zlo")
    core = lax.axis_index("core")
    cores = lax.axis_size("core")
    mine = chip * cores + core
    remote = lax.ppermute(out_weight, "zlo", pair)
    neighbour = lax.ppermute(out_weight, "core", pair)
    relayed = lax.ppermute(remote, "core", pair)
    other_chip = (1 - chip) * cores
    return [
        (mine, out_weight),
        (chip * cores + 1 - core, neighbour),
        (other_chip + core, remote),
        (other_chip + 1 - core, relayed),
    ]


def scan_shifts(count):
    first = [1, 2] if count > 2 else [1]
    later = []
    span = 2
    while span < count:
        later.append(span)
        span *= 2
    return first, later


def scan_kernel(count, ending_ref, decay_ref, entering_ref, sent, landed, send_sem, recv_sem):
    me = lax.axis_index("ctx")
    first, later = scan_shifts(count)
    partners = sorted(set(first + later))

    barrier = pltpu.get_barrier_semaphore()
    for span in partners:
        for target in (lax.rem(me + span, count), lax.rem(me + count - span, count)):
            pl.semaphore_signal(barrier, inc=1, device_id={"ctx": target}, device_id_type=pl.DeviceIdType.MESH)
    pl.semaphore_wait(barrier, 2 * len(partners))

    def send(source, slot, span):
        copy = pltpu.make_async_remote_copy(
            src_ref=source,
            dst_ref=landed.at[slot],
            send_sem=send_sem.at[slot],
            recv_sem=recv_sem.at[slot],
            device_id={"ctx": lax.rem(me + span, count)},
            device_id_type=pl.DeviceIdType.MESH,
        )
        copy.start()
        return copy

    def arrived(slot, span):
        return jnp.where(me >= span, landed[slot], 0.0)

    copies = [send(ending_ref, slot, span) for slot, span in enumerate(first)]
    for copy in copies:
        copy.wait_recv()
    total = arrived(0, first[0])
    if len(first) > 1:
        total = total + decay_ref[0] * arrived(1, first[1])
    for step, span in enumerate(later):
        slot = len(first) + step
        sent[step] = total
        copies.append(send(sent.at[step], slot, span))
        copies[-1].wait_recv()
        total = total + decay_ref[step + 1] * arrived(slot, span)
    entering_ref[...] = total
    for copy in copies:
        copy.wait_send()


def scan_states(ending, decay):
    count = lax.axis_size("ctx")
    first, later = scan_shifts(count)
    slots = len(first) + len(later)
    vmem = pl.BlockSpec(memory_space=pltpu.VMEM)
    return pl.pallas_call(
        functools.partial(scan_kernel, count),
        out_shape=jax.ShapeDtypeStruct(ending.shape, jnp.float32),
        in_specs=[vmem, vmem],
        out_specs=vmem,
        scratch_shapes=[
            pltpu.VMEM((max(1, len(later)),) + ending.shape, jnp.float32),
            pltpu.VMEM((slots,) + ending.shape, jnp.float32),
            pltpu.SemaphoreType.DMA((slots,)),
            pltpu.SemaphoreType.DMA((slots,)),
        ],
        compiler_params=pltpu.CompilerParams(collective_id=0, has_side_effects=True),
    )(ending, decay)


def local(query_in, key_in, value_in, feature_taps, decay_rate, residues, skip_gain, out_weight):
    weight_blocks = gather_weight(out_weight)
    query_rows = query_in[0]
    key_rows = key_in[0]
    value_rows = value_in[0]
    rows_here, chans = query_rows.shape
    keep = FEAT - 1
    tails = shifted(
        jnp.concatenate(
            [query_rows[rows_here - keep :], key_rows[rows_here - keep :], value_rows[rows_here - keep :]],
            axis=0,
        ),
        "ctx",
        1,
    )
    featured_q = featurize(query_rows, tails[0:keep], feature_taps[0])
    featured_k = featurize(key_rows, tails[keep : 2 * keep], feature_taps[1])
    featured_v = featurize(value_rows, tails[2 * keep :], feature_taps[2])
    kv_round = (featured_k * featured_v).astype(jnp.bfloat16)

    groups = chans // GROUP
    width = rows_here
    kv_grouped = kv_round.reshape(width, groups, GROUP)

    positions = jnp.arange(width, dtype=jnp.float32)
    scale = residues * jnp.sqrt(-jnp.expm1(-2.0 * decay_rate))
    powers = jnp.exp(-decay_rate[:, :, None] * positions)
    kernel = jnp.einsum("gm,gmt->gt", scale, powers, precision=exact_precision)
    closing = jnp.exp(-decay_rate[:, :, None] * (width - 1.0 - positions))
    lagged = jnp.exp(-decay_rate[:, :, None] * (positions + 1.0)) * scale[:, :, None]

    high, low = toeplitz(kernel)
    inner = jnp.einsum("gij,jgc->igc", high, kv_grouped, preferred_element_type=jnp.float32)
    inner = inner + jnp.einsum("gij,jgc->igc", low, kv_grouped, preferred_element_type=jnp.float32)
    ending = two_pass("gnj,jgc->ngc", closing, kv_grouped).reshape(-1, chans)

    first, later = scan_shifts(lax.axis_size("ctx"))
    spans = jnp.asarray([1] * (len(first) - 1) + later, jnp.float32)[:, None, None] * float(width)
    modes = decay_rate.shape[1]
    rate_lanes = jnp.broadcast_to(jnp.transpose(decay_rate)[:, :, None], (modes, groups, GROUP))
    decay = jnp.exp(-rate_lanes.reshape(1, modes, chans) * spans)
    entering = scan_states(ending, decay).reshape(-1, groups, GROUP)
    crossing = jnp.einsum("gni,ngc->igc", lagged, entering, precision=exact_precision)
    convolved = (inner + crossing).reshape(width, chans).astype(jnp.bfloat16)

    gated = (
        featured_q * (convolved.astype(jnp.float32) + skip_gain * kv_round.astype(jnp.float32))
    ).astype(jnp.bfloat16)
    rows = out_weight.shape[0]
    block_out = None
    for owner, weight in weight_blocks:
        columns = lax.dynamic_slice_in_dim(gated, owner * rows, rows, axis=1)
        term = jnp.dot(columns, weight, preferred_element_type=jnp.float32)
        block_out = term if block_out is None else block_out + term
    return block_out.astype(jnp.bfloat16)[None]


def solution(mesh):
    ctx_size, fsdp_size = mesh.shape["ctx"], mesh.shape["fsdp"]
    split = jax.sharding.Mesh(
        mesh.devices.reshape(ctx_size, fsdp_size // 2, 2), ("ctx", "zlo", "core")
    )
    batch = ("zlo", "core")
    return jax.shard_map(
        local,
        mesh=split,
        in_specs=(
            P(batch, "ctx", None),
            P(batch, "ctx", None),
            P(batch, "ctx", None),
            P(),
            P(),
            P(),
            P(),
            P(batch, None),
        ),
        out_specs=P(batch, "ctx", None),
        check_vma=False,
    )
```

```python
import functools

import jax
import jax.numpy as jnp
from jax import lax
from jax.experimental import pallas as pl
from jax.experimental.pallas import tpu as pltpu
from jax.sharding import PartitionSpec as P

GROUP = 16
FEAT = 3

exact_precision = lax.Precision.HIGHEST


def shifted(shard, axis, by):
    count = lax.axis_size(axis)
    pairs = [(i, i + by) for i in range(count) if 0 <= i + by < count]
    return lax.ppermute(shard, axis, pairs)


def featurize(rows, tail, taps_one):
    values = jnp.concatenate([tail, rows], axis=0).astype(jnp.float32)
    count = rows.shape[0]
    total = taps_one[0] * values[FEAT - 1 :]
    for offset in range(1, FEAT):
        total = total + taps_one[offset] * values[FEAT - 1 - offset : FEAT - 1 - offset + count]
    return total


def split_bf16(values):
    rounded = lax.reduce_precision(values, exponent_bits=8, mantissa_bits=7)
    return rounded.astype(jnp.bfloat16), (values - rounded).astype(jnp.bfloat16)


def two_pass(spec, table, signal):
    high, low = split_bf16(table)
    first = jnp.einsum(spec, high, signal, preferred_element_type=jnp.float32)
    return first + jnp.einsum(spec, low, signal, preferred_element_type=jnp.float32)


def toeplitz(kernel):
    width = kernel.shape[1]
    lag = lax.optimization_barrier(jnp.arange(width, dtype=jnp.int32))
    diff = lag[:, None] - lag[None, :]
    onehot = (lag[:, None, None] == diff[None, :, :]).astype(jnp.bfloat16)
    return [
        jnp.einsum("gs,sij->gij", part, onehot, preferred_element_type=jnp.bfloat16)
        for part in split_bf16(kernel)
    ]


def gather_weight(out_weight):
    pair = [(0, 1), (1, 0)]
    chip = lax.axis_index("zlo")
    core = lax.axis_index("core")
    cores = lax.axis_size("core")
    mine = chip * cores + core
    remote = lax.ppermute(out_weight, "zlo", pair)
    neighbour = lax.ppermute(out_weight, "core", pair)
    relayed = lax.ppermute(remote, "core", pair)
    other_chip = (1 - chip) * cores
    return [
        (mine, out_weight),
        (chip * cores + 1 - core, neighbour),
        (other_chip + core, remote),
        (other_chip + 1 - core, relayed),
    ]


def scan_shifts(count):
    first = [1, 2] if count > 2 else [1]
    later = []
    span = 2
    while span < count:
        later.append(span)
        span *= 2
    return first, later


def scan_kernel(count, ending_ref, decay_ref, entering_ref, sent, landed, send_sem, recv_sem):
    me = lax.axis_index("ctx")
    first, later = scan_shifts(count)
    partners = sorted(set(first + later))

    barrier = pltpu.get_barrier_semaphore()
    for span in partners:
        for target in (lax.rem(me + span, count), lax.rem(me + count - span, count)):
            pl.semaphore_signal(barrier, inc=1, device_id={"ctx": target}, device_id_type=pl.DeviceIdType.MESH)
    pl.semaphore_wait(barrier, 2 * len(partners))

    copies = []

    def send(source, slot, span):
        copy = pltpu.make_async_remote_copy(
            src_ref=source,
            dst_ref=landed.at[slot],
            send_sem=send_sem.at[slot],
            recv_sem=recv_sem.at[slot],
            device_id={"ctx": lax.rem(me + span, count)},
            device_id_type=pl.DeviceIdType.MESH,
        )

        @pl.when(me + span < count)
        def _():
            copy.start()

        copies.append((copy, span))
        return copy

    def take(copy, slot, span, factor):
        @pl.when(me >= span)
        def _():
            copy.wait_recv()
            if factor is None:
                entering_ref[...] += landed[slot]
            else:
                entering_ref[...] += factor * landed[slot]

    entering_ref[...] = jnp.zeros(entering_ref.shape, jnp.float32)
    opening = [send(ending_ref, slot, span) for slot, span in enumerate(first)]
    for slot, span in enumerate(first):
        take(opening[slot], slot, span, None if slot == 0 else decay_ref[0])
    for step, span in enumerate(later):
        slot = len(first) + step
        sent[step] = entering_ref[...]
        copy = send(sent.at[step], slot, span)
        take(copy, slot, span, decay_ref[step + 1])
    for copy, span in copies:

        @pl.when(me + span < count)
        def _():
            copy.wait_send()


def scan_states(ending, decay):
    count = lax.axis_size("ctx")
    first, later = scan_shifts(count)
    slots = len(first) + len(later)
    vmem = pl.BlockSpec(memory_space=pltpu.VMEM)
    return pl.pallas_call(
        functools.partial(scan_kernel, count),
        out_shape=jax.ShapeDtypeStruct(ending.shape, jnp.float32),
        in_specs=[vmem, vmem],
        out_specs=vmem,
        scratch_shapes=[
            pltpu.VMEM((max(1, len(later)),) + ending.shape, jnp.float32),
            pltpu.VMEM((slots,) + ending.shape, jnp.float32),
            pltpu.SemaphoreType.DMA((slots,)),
            pltpu.SemaphoreType.DMA((slots,)),
        ],
        compiler_params=pltpu.CompilerParams(collective_id=0, has_side_effects=True),
    )(ending, decay)


def local(query_in, key_in, value_in, feature_taps, decay_rate, residues, skip_gain, out_weight):
    weight_blocks = gather_weight(out_weight)
    query_rows = query_in[0]
    key_rows = key_in[0]
    value_rows = value_in[0]
    rows_here, chans = query_rows.shape
    keep = FEAT - 1
    tails = shifted(
        jnp.concatenate(
            [query_rows[rows_here - keep :], key_rows[rows_here - keep :], value_rows[rows_here - keep :]],
            axis=0,
        ),
        "ctx",
        1,
    )
    featured_q = featurize(query_rows, tails[0:keep], feature_taps[0])
    featured_k = featurize(key_rows, tails[keep : 2 * keep], feature_taps[1])
    featured_v = featurize(value_rows, tails[2 * keep :], feature_taps[2])
    kv_round = (featured_k * featured_v).astype(jnp.bfloat16)

    groups = chans // GROUP
    width = rows_here
    kv_grouped = kv_round.reshape(width, groups, GROUP)

    positions = jnp.arange(width, dtype=jnp.float32)
    scale = residues * jnp.sqrt(-jnp.expm1(-2.0 * decay_rate))
    powers = jnp.exp(-decay_rate[:, :, None] * positions)
    kernel = jnp.einsum("gm,gmt->gt", scale, powers, precision=exact_precision)
    closing = jnp.exp(-decay_rate[:, :, None] * (width - 1.0 - positions))
    lagged = jnp.exp(-decay_rate[:, :, None] * (positions + 1.0)) * scale[:, :, None]

    high, low = toeplitz(kernel)
    inner = jnp.einsum("gij,jgc->igc", high, kv_grouped, preferred_element_type=jnp.float32)
    inner = inner + jnp.einsum("gij,jgc->igc", low, kv_grouped, preferred_element_type=jnp.float32)
    ending = two_pass("gnj,jgc->ngc", closing, kv_grouped).reshape(-1, chans)

    first, later = scan_shifts(lax.axis_size("ctx"))
    spans = jnp.asarray([1] * (len(first) - 1) + later, jnp.float32)[:, None, None] * float(width)
    modes = decay_rate.shape[1]
    rate_lanes = jnp.broadcast_to(jnp.transpose(decay_rate)[:, :, None], (modes, groups, GROUP))
    decay = jnp.exp(-rate_lanes.reshape(1, modes, chans) * spans)
    entering = scan_states(ending, decay).reshape(-1, groups, GROUP)
    crossing = jnp.einsum("gni,ngc->igc", lagged, entering, precision=exact_precision)
    convolved = (inner + crossing).reshape(width, chans).astype(jnp.bfloat16)

    gated = (
        featured_q * (convolved.astype(jnp.float32) + skip_gain * kv_round.astype(jnp.float32))
    ).astype(jnp.bfloat16)
    rows = out_weight.shape[0]
    block_out = None
    for owner, weight in weight_blocks:
        columns = lax.dynamic_slice_in_dim(gated, owner * rows, rows, axis=1)
        term = jnp.dot(columns, weight, preferred_element_type=jnp.float32)
        block_out = term if block_out is None else block_out + term
    return block_out.astype(jnp.bfloat16)[None]


def solution(mesh):
    ctx_size, fsdp_size = mesh.shape["ctx"], mesh.shape["fsdp"]
    split = jax.sharding.Mesh(
        mesh.devices.reshape(ctx_size, fsdp_size // 2, 2), ("ctx", "zlo", "core")
    )
    batch = ("zlo", "core")
    return jax.shard_map(
        local,
        mesh=split,
        in_specs=(
            P(batch, "ctx", None),
            P(batch, "ctx", None),
            P(batch, "ctx", None),
            P(),
            P(),
            P(),
            P(),
            P(batch, None),
        ),
        out_specs=P(batch, "ctx", None),
        check_vma=False,
    )
```

```python
import functools

import jax
import jax.numpy as jnp
from jax import lax
from jax.experimental import pallas as pl
from jax.experimental.pallas import tpu as pltpu
from jax.sharding import PartitionSpec as P

GROUP = 16
FEAT = 3

exact_precision = lax.Precision.HIGHEST


def shifted(shard, axis, by):
    count = lax.axis_size(axis)
    pairs = [(i, i + by) for i in range(count) if 0 <= i + by < count]
    return lax.ppermute(shard, axis, pairs)


def featurize(rows, tail, taps_one):
    values = jnp.concatenate([tail, rows], axis=0).astype(jnp.float32)
    count = rows.shape[0]
    total = taps_one[0] * values[FEAT - 1 :]
    for offset in range(1, FEAT):
        total = total + taps_one[offset] * values[FEAT - 1 - offset : FEAT - 1 - offset + count]
    return total


def split_bf16(values):
    rounded = lax.reduce_precision(values, exponent_bits=8, mantissa_bits=7)
    return rounded.astype(jnp.bfloat16), (values - rounded).astype(jnp.bfloat16)


def two_pass(spec, table, signal):
    high, low = split_bf16(table)
    first = jnp.einsum(spec, high, signal, preferred_element_type=jnp.float32)
    return first + jnp.einsum(spec, low, signal, preferred_element_type=jnp.float32)


def toeplitz(kernel):
    width = kernel.shape[1]
    lag = lax.optimization_barrier(jnp.arange(width, dtype=jnp.int32))
    diff = lag[:, None] - lag[None, :]
    onehot = (lag[:, None, None] == diff[None, :, :]).astype(jnp.bfloat16)
    return [
        jnp.einsum("gs,sij->gij", part, onehot, preferred_element_type=jnp.bfloat16)
        for part in split_bf16(kernel)
    ]


def gather_weight(out_weight):
    pair = [(0, 1), (1, 0)]
    chip = lax.axis_index("zlo")
    core = lax.axis_index("core")
    cores = lax.axis_size("core")
    mine = chip * cores + core
    remote = lax.ppermute(out_weight, "zlo", pair)
    neighbour = lax.ppermute(out_weight, "core", pair)
    relayed = lax.ppermute(remote, "core", pair)
    other_chip = (1 - chip) * cores
    return [
        (mine, out_weight),
        (chip * cores + 1 - core, neighbour),
        (other_chip + core, remote),
        (other_chip + 1 - core, relayed),
    ]


def scan_shifts(count):
    first = [1, 2] if count > 2 else [1]
    later = []
    span = 2
    while span < count:
        later.append(span)
        span *= 2
    return first, later


def conv_tiles(high_ref, low_ref, kv_ref, inner_ref, first_tile, last_tile):
    lanes = kv_ref.shape[0]
    per_tile = 128 // GROUP
    owner = lax.broadcasted_iota(jnp.int32, (1, 128), 1) // GROUP

    def body(tile, carry):
        col = pl.multiple_of(tile * 128, 128)
        block = kv_ref[:, pl.ds(col, 128)]
        total = jnp.zeros((lanes, 128), jnp.float32)
        for member in range(per_tile):
            group = tile * per_tile + member
            part = jnp.where(owner == member, block, jnp.zeros_like(block))
            total += jnp.dot(high_ref[group], part, preferred_element_type=jnp.float32)
            total += jnp.dot(low_ref[group], part, preferred_element_type=jnp.float32)
        inner_ref[:, pl.ds(col, 128)] = total
        return carry

    lax.fori_loop(first_tile, last_tile, body, 0)


def scan_kernel(
    count, ending_ref, decay_ref, high_ref, low_ref, kv_ref, entering_ref, inner_ref, sent, landed, send_sem, recv_sem
):
    me = lax.axis_index("ctx")
    first, later = scan_shifts(count)
    partners = sorted(set(first + later))

    barrier = pltpu.get_barrier_semaphore()
    for span in partners:
        for target in (lax.rem(me + span, count), lax.rem(me + count - span, count)):
            pl.semaphore_signal(barrier, inc=1, device_id={"ctx": target}, device_id_type=pl.DeviceIdType.MESH)
    pl.semaphore_wait(barrier, 2 * len(partners))

    copies = []

    def send(source, slot, span):
        copy = pltpu.make_async_remote_copy(
            src_ref=source,
            dst_ref=landed.at[slot],
            send_sem=send_sem.at[slot],
            recv_sem=recv_sem.at[slot],
            device_id={"ctx": lax.rem(me + span, count)},
            device_id_type=pl.DeviceIdType.MESH,
        )

        @pl.when(me + span < count)
        def _():
            copy.start()

        copies.append((copy, span))
        return copy

    def take(copy, slot, span, factor):
        @pl.when(me >= span)
        def _():
            copy.wait_recv()
            if factor is None:
                entering_ref[...] += landed[slot]
            else:
                entering_ref[...] += factor * landed[slot]

    tiles = kv_ref.shape[1] // 128
    rounds = 1 + len(later)
    bounds = [tiles * step // rounds for step in range(rounds + 1)]

    entering_ref[...] = jnp.zeros(entering_ref.shape, jnp.float32)
    opening = [send(ending_ref, slot, span) for slot, span in enumerate(first)]
    conv_tiles(high_ref, low_ref, kv_ref, inner_ref, bounds[0], bounds[1])
    for slot, span in enumerate(first):
        take(opening[slot], slot, span, None if slot == 0 else decay_ref[0])
    for step, span in enumerate(later):
        slot = len(first) + step
        sent[step] = entering_ref[...]
        copy = send(sent.at[step], slot, span)
        conv_tiles(high_ref, low_ref, kv_ref, inner_ref, bounds[step + 1], bounds[step + 2])
        take(copy, slot, span, decay_ref[step + 1])
    for copy, span in copies:

        @pl.when(me + span < count)
        def _():
            copy.wait_send()


def scan_states(ending, decay, high, low, kv):
    count = lax.axis_size("ctx")
    first, later = scan_shifts(count)
    slots = len(first) + len(later)
    vmem = pl.BlockSpec(memory_space=pltpu.VMEM)
    return pl.pallas_call(
        functools.partial(scan_kernel, count),
        out_shape=(
            jax.ShapeDtypeStruct(ending.shape, jnp.float32),
            jax.ShapeDtypeStruct(kv.shape, jnp.float32),
        ),
        in_specs=[vmem] * 5,
        out_specs=(vmem, vmem),
        scratch_shapes=[
            pltpu.VMEM((max(1, len(later)),) + ending.shape, jnp.float32),
            pltpu.VMEM((slots,) + ending.shape, jnp.float32),
            pltpu.SemaphoreType.DMA((slots,)),
            pltpu.SemaphoreType.DMA((slots,)),
        ],
        compiler_params=pltpu.CompilerParams(
            collective_id=0, has_side_effects=True, vmem_limit_bytes=48 * 1024 * 1024
        ),
    )(ending, decay, high, low, kv)


def local(query_in, key_in, value_in, feature_taps, decay_rate, residues, skip_gain, out_weight):
    weight_blocks = gather_weight(out_weight)
    query_rows = query_in[0]
    key_rows = key_in[0]
    value_rows = value_in[0]
    rows_here, chans = query_rows.shape
    keep = FEAT - 1
    tails = shifted(
        jnp.concatenate(
            [query_rows[rows_here - keep :], key_rows[rows_here - keep :], value_rows[rows_here - keep :]],
            axis=0,
        ),
        "ctx",
        1,
    )
    featured_q = featurize(query_rows, tails[0:keep], feature_taps[0])
    featured_k = featurize(key_rows, tails[keep : 2 * keep], feature_taps[1])
    featured_v = featurize(value_rows, tails[2 * keep :], feature_taps[2])
    kv_round = (featured_k * featured_v).astype(jnp.bfloat16)

    groups = chans // GROUP
    width = rows_here
    kv_grouped = kv_round.reshape(width, groups, GROUP)

    positions = jnp.arange(width, dtype=jnp.float32)
    scale = residues * jnp.sqrt(-jnp.expm1(-2.0 * decay_rate))
    powers = jnp.exp(-decay_rate[:, :, None] * positions)
    kernel = jnp.einsum("gm,gmt->gt", scale, powers, precision=exact_precision)
    closing = jnp.exp(-decay_rate[:, :, None] * (width - 1.0 - positions))
    lagged = jnp.exp(-decay_rate[:, :, None] * (positions + 1.0)) * scale[:, :, None]

    high, low = toeplitz(kernel)
    ending = two_pass("gnj,jgc->ngc", closing, kv_grouped).reshape(-1, chans)

    first, later = scan_shifts(lax.axis_size("ctx"))
    spans = jnp.asarray([1] * (len(first) - 1) + later, jnp.float32)[:, None, None] * float(width)
    modes = decay_rate.shape[1]
    rate_lanes = jnp.broadcast_to(jnp.transpose(decay_rate)[:, :, None], (modes, groups, GROUP))
    decay = jnp.exp(-rate_lanes.reshape(1, modes, chans) * spans)
    entering, inner = scan_states(ending, decay, high, low, kv_round)
    entering = entering.reshape(-1, groups, GROUP)
    crossing = jnp.einsum("gni,ngc->igc", lagged, entering, precision=exact_precision)
    convolved = (inner + crossing.reshape(width, chans)).astype(jnp.bfloat16)

    gated = (
        featured_q * (convolved.astype(jnp.float32) + skip_gain * kv_round.astype(jnp.float32))
    ).astype(jnp.bfloat16)
    rows = out_weight.shape[0]
    block_out = None
    for owner, weight in weight_blocks:
        columns = lax.dynamic_slice_in_dim(gated, owner * rows, rows, axis=1)
        term = jnp.dot(columns, weight, preferred_element_type=jnp.float32)
        block_out = term if block_out is None else block_out + term
    return block_out.astype(jnp.bfloat16)[None]


def solution(mesh):
    ctx_size, fsdp_size = mesh.shape["ctx"], mesh.shape["fsdp"]
    split = jax.sharding.Mesh(
        mesh.devices.reshape(ctx_size, fsdp_size // 2, 2), ("ctx", "zlo", "core")
    )
    batch = ("zlo", "core")
    return jax.shard_map(
        local,
        mesh=split,
        in_specs=(
            P(batch, "ctx", None),
            P(batch, "ctx", None),
            P(batch, "ctx", None),
            P(),
            P(),
            P(),
            P(),
            P(batch, None),
        ),
        out_specs=P(batch, "ctx", None),
        check_vma=False,
    )
```

```python
import functools

import jax
import jax.numpy as jnp
from jax import lax
from jax.experimental import pallas as pl
from jax.experimental.pallas import tpu as pltpu
from jax.sharding import PartitionSpec as P

GROUP = 16
FEAT = 3

exact_precision = lax.Precision.HIGHEST


def shifted(shard, axis, by):
    count = lax.axis_size(axis)
    pairs = [(i, i + by) for i in range(count) if 0 <= i + by < count]
    return lax.ppermute(shard, axis, pairs)


def featurize(rows, tail, taps_one):
    values = jnp.concatenate([tail, rows], axis=0).astype(jnp.float32)
    count = rows.shape[0]
    total = taps_one[0] * values[FEAT - 1 :]
    for offset in range(1, FEAT):
        total = total + taps_one[offset] * values[FEAT - 1 - offset : FEAT - 1 - offset + count]
    return total


def split_bf16(values):
    rounded = lax.reduce_precision(values, exponent_bits=8, mantissa_bits=7)
    return rounded.astype(jnp.bfloat16), (values - rounded).astype(jnp.bfloat16)


def two_pass(spec, table, signal):
    high, low = split_bf16(table)
    first = jnp.einsum(spec, high, signal, preferred_element_type=jnp.float32)
    return first + jnp.einsum(spec, low, signal, preferred_element_type=jnp.float32)


def scan_shifts(count):
    first = [1, 2] if count > 2 else [1]
    later = []
    span = 2
    while span < count:
        later.append(span)
        span *= 2
    return first, later


def conv_tiles(high_ref, low_ref, kv_ref, inner_ref, first_tile, last_tile):
    width = kv_ref.shape[0]
    per_tile = 128 // GROUP
    owner = lax.broadcasted_iota(jnp.int32, (1, 128), 1) // GROUP
    causal = lax.broadcasted_iota(jnp.int32, (width, width), 1) <= lax.broadcasted_iota(
        jnp.int32, (width, width), 0
    )

    def toeplitz_part(ref, group):
        row = ref[pl.ds(group, 1), :]
        rolled = pltpu.roll(jnp.broadcast_to(row, (width, width)), 0, 1, stride=1, stride_axis=0)
        return jnp.where(causal, rolled, 0.0).astype(jnp.bfloat16)

    def body(tile, carry):
        col = pl.multiple_of(tile * 128, 128)
        block = kv_ref[:, pl.ds(col, 128)]
        total = jnp.zeros((width, 128), jnp.float32)
        for member in range(per_tile):
            group = tile * per_tile + member
            part = jnp.where(owner == member, block, jnp.zeros_like(block))
            total += jnp.dot(toeplitz_part(high_ref, group), part, preferred_element_type=jnp.float32)
            total += jnp.dot(toeplitz_part(low_ref, group), part, preferred_element_type=jnp.float32)
        inner_ref[:, pl.ds(col, 128)] = total
        return carry

    lax.fori_loop(first_tile, last_tile, body, 0)


def scan_kernel(
    count, ending_ref, decay_ref, high_ref, low_ref, kv_ref, entering_ref, inner_ref, sent, landed, send_sem, recv_sem
):
    me = lax.axis_index("ctx")
    first, later = scan_shifts(count)
    partners = sorted(set(first + later))

    barrier = pltpu.get_barrier_semaphore()
    for span in partners:
        for target in (lax.rem(me + span, count), lax.rem(me + count - span, count)):
            pl.semaphore_signal(barrier, inc=1, device_id={"ctx": target}, device_id_type=pl.DeviceIdType.MESH)
    pl.semaphore_wait(barrier, 2 * len(partners))

    copies = []

    def send(source, slot, span):
        copy = pltpu.make_async_remote_copy(
            src_ref=source,
            dst_ref=landed.at[slot],
            send_sem=send_sem.at[slot],
            recv_sem=recv_sem.at[slot],
            device_id={"ctx": lax.rem(me + span, count)},
            device_id_type=pl.DeviceIdType.MESH,
        )

        @pl.when(me + span < count)
        def _():
            copy.start()

        copies.append((copy, span))
        return copy

    def take(copy, slot, span, factor):
        @pl.when(me >= span)
        def _():
            copy.wait_recv()
            if factor is None:
                entering_ref[...] += landed[slot]
            else:
                entering_ref[...] += factor * landed[slot]

    tiles = kv_ref.shape[1] // 128
    rounds = 1 + len(later)
    bounds = [tiles * step // rounds for step in range(rounds + 1)]

    entering_ref[...] = jnp.zeros(entering_ref.shape, jnp.float32)
    opening = [send(ending_ref, slot, span) for slot, span in enumerate(first)]
    conv_tiles(high_ref, low_ref, kv_ref, inner_ref, bounds[0], bounds[1])
    for slot, span in enumerate(first):
        take(opening[slot], slot, span, None if slot == 0 else decay_ref[0])
    for step, span in enumerate(later):
        slot = len(first) + step
        sent[step] = entering_ref[...]
        copy = send(sent.at[step], slot, span)
        conv_tiles(high_ref, low_ref, kv_ref, inner_ref, bounds[step + 1], bounds[step + 2])
        take(copy, slot, span, decay_ref[step + 1])
    for copy, span in copies:

        @pl.when(me + span < count)
        def _():
            copy.wait_send()


def scan_states(ending, decay, high, low, kv):
    count = lax.axis_size("ctx")
    first, later = scan_shifts(count)
    slots = len(first) + len(later)
    vmem = pl.BlockSpec(memory_space=pltpu.VMEM)
    return pl.pallas_call(
        functools.partial(scan_kernel, count),
        out_shape=(
            jax.ShapeDtypeStruct(ending.shape, jnp.float32),
            jax.ShapeDtypeStruct(kv.shape, jnp.float32),
        ),
        in_specs=[vmem] * 5,
        out_specs=(vmem, vmem),
        scratch_shapes=[
            pltpu.VMEM((max(1, len(later)),) + ending.shape, jnp.float32),
            pltpu.VMEM((slots,) + ending.shape, jnp.float32),
            pltpu.SemaphoreType.DMA((slots,)),
            pltpu.SemaphoreType.DMA((slots,)),
        ],
        compiler_params=pltpu.CompilerParams(
            collective_id=0, has_side_effects=True, vmem_limit_bytes=48 * 1024 * 1024
        ),
    )(ending, decay, high, low, kv)


def local(query_in, key_in, value_in, feature_taps, decay_rate, residues, skip_gain, out_weight):
    pair = [(0, 1), (1, 0)]
    chip = lax.axis_index("zlo")
    core = lax.axis_index("core")
    cores = lax.axis_size("core")
    other_chip = (1 - chip) * cores
    remote = lax.ppermute(out_weight, "zlo", pair)
    weight_blocks = [
        (chip * cores + core, out_weight),
        (chip * cores + 1 - core, lax.ppermute(out_weight, "core", pair)),
        (other_chip + core, remote),
    ]
    query_rows = query_in[0]
    key_rows = key_in[0]
    value_rows = value_in[0]
    rows_here, chans = query_rows.shape
    keep = FEAT - 1
    tails = shifted(
        jnp.concatenate(
            [query_rows[rows_here - keep :], key_rows[rows_here - keep :], value_rows[rows_here - keep :]],
            axis=0,
        ),
        "ctx",
        1,
    )
    featured_q = featurize(query_rows, tails[0:keep], feature_taps[0])
    featured_k = featurize(key_rows, tails[keep : 2 * keep], feature_taps[1])
    featured_v = featurize(value_rows, tails[2 * keep :], feature_taps[2])
    kv_round = (featured_k * featured_v).astype(jnp.bfloat16)

    groups = chans // GROUP
    width = rows_here
    kv_grouped = kv_round.reshape(width, groups, GROUP)

    positions = jnp.arange(width, dtype=jnp.float32)
    scale = residues * jnp.sqrt(-jnp.expm1(-2.0 * decay_rate))
    powers = jnp.exp(-decay_rate[:, :, None] * positions)
    kernel = jnp.einsum("gm,gmt->gt", scale, powers, precision=exact_precision)
    closing = jnp.exp(-decay_rate[:, :, None] * (width - 1.0 - positions))
    lagged = jnp.exp(-decay_rate[:, :, None] * (positions + 1.0)) * scale[:, :, None]

    taps = jnp.roll(kernel[:, ::-1], 1, axis=1)
    high = lax.reduce_precision(taps, exponent_bits=8, mantissa_bits=7)
    low = lax.reduce_precision(taps - high, exponent_bits=8, mantissa_bits=7)
    ending = two_pass("gnj,jgc->ngc", closing, kv_grouped).reshape(-1, chans)

    first, later = scan_shifts(lax.axis_size("ctx"))
    spans = jnp.asarray([1] * (len(first) - 1) + later, jnp.float32)[:, None, None] * float(width)
    modes = decay_rate.shape[1]
    rate_lanes = jnp.broadcast_to(jnp.transpose(decay_rate)[:, :, None], (modes, groups, GROUP))
    decay = jnp.exp(-rate_lanes.reshape(1, modes, chans) * spans)
    entering, inner = scan_states(ending, decay, high, low, kv_round)
    entering, remote = lax.optimization_barrier((entering, remote))
    weight_blocks.append((other_chip + 1 - core, lax.ppermute(remote, "core", [(0, 1), (1, 0)])))
    entering = entering.reshape(-1, groups, GROUP)
    crossing = jnp.einsum("gni,ngc->igc", lagged, entering, precision=exact_precision)
    convolved = (inner + crossing.reshape(width, chans)).astype(jnp.bfloat16)

    gated = (
        featured_q * (convolved.astype(jnp.float32) + skip_gain * kv_round.astype(jnp.float32))
    ).astype(jnp.bfloat16)
    rows = out_weight.shape[0]
    block_out = None
    for owner, weight in weight_blocks:
        columns = lax.dynamic_slice_in_dim(gated, owner * rows, rows, axis=1)
        term = jnp.dot(columns, weight, preferred_element_type=jnp.float32)
        block_out = term if block_out is None else block_out + term
    return block_out.astype(jnp.bfloat16)[None]


def solution(mesh):
    ctx_size, fsdp_size = mesh.shape["ctx"], mesh.shape["fsdp"]
    split = jax.sharding.Mesh(
        mesh.devices.reshape(ctx_size, fsdp_size // 2, 2), ("ctx", "zlo", "core")
    )
    batch = ("zlo", "core")
    return jax.shard_map(
        local,
        mesh=split,
        in_specs=(
            P(batch, "ctx", None),
            P(batch, "ctx", None),
            P(batch, "ctx", None),
            P(),
            P(),
            P(),
            P(),
            P(batch, None),
        ),
        out_specs=P(batch, "ctx", None),
        check_vma=False,
    )
```

```python
import functools

import jax
import jax.numpy as jnp
from jax import lax
from jax.experimental import pallas as pl
from jax.experimental.pallas import tpu as pltpu
from jax.sharding import PartitionSpec as P

GROUP = 16
FEAT = 3

exact_precision = lax.Precision.HIGHEST


def shifted(shard, axis, by):
    count = lax.axis_size(axis)
    pairs = [(i, i + by) for i in range(count) if 0 <= i + by < count]
    return lax.ppermute(shard, axis, pairs)


def featurize(rows, tail, taps_one):
    values = jnp.concatenate([tail, rows], axis=0).astype(jnp.float32)
    count = rows.shape[0]
    total = taps_one[0] * values[FEAT - 1 :]
    for offset in range(1, FEAT):
        total = total + taps_one[offset] * values[FEAT - 1 - offset : FEAT - 1 - offset + count]
    return total


def split_bf16(values):
    rounded = lax.reduce_precision(values, exponent_bits=8, mantissa_bits=7)
    return rounded.astype(jnp.bfloat16), (values - rounded).astype(jnp.bfloat16)


def two_pass(spec, table, signal):
    high, low = split_bf16(table)
    first = jnp.einsum(spec, high, signal, preferred_element_type=jnp.float32)
    return first + jnp.einsum(spec, low, signal, preferred_element_type=jnp.float32)


def scan_shifts(count):
    first = [1, 2] if count > 2 else [1]
    later = []
    span = 2
    while span < count:
        later.append(span)
        span *= 2
    return first, later


def conv_tiles(high_ref, low_ref, kv_ref, inner_ref, first_tile, last_tile):
    width = kv_ref.shape[0]
    per_tile = 128 // GROUP
    owner = lax.broadcasted_iota(jnp.int32, (1, 128), 1) // GROUP
    causal = lax.broadcasted_iota(jnp.int32, (width, width), 1) <= lax.broadcasted_iota(
        jnp.int32, (width, width), 0
    )

    def toeplitz_part(ref, group):
        row = ref[pl.ds(group, 1), :]
        rolled = pltpu.roll(jnp.broadcast_to(row, (width, width)), 0, 1, stride=1, stride_axis=0)
        return jnp.where(causal, rolled, 0.0).astype(jnp.bfloat16)

    def body(tile, carry):
        col = pl.multiple_of(tile * 128, 128)
        block = kv_ref[:, pl.ds(col, 128)]
        total = jnp.zeros((width, 128), jnp.float32)
        for member in range(per_tile):
            group = tile * per_tile + member
            part = jnp.where(owner == member, block, jnp.zeros_like(block))
            total += jnp.dot(toeplitz_part(high_ref, group), part, preferred_element_type=jnp.float32)
            total += jnp.dot(toeplitz_part(low_ref, group), part, preferred_element_type=jnp.float32)
        inner_ref[:, pl.ds(col, 128)] = total
        return carry

    lax.fori_loop(first_tile, last_tile, body, 0)


def scan_kernel(
    count, parts, ending_ref, decay_ref, high_ref, low_ref, kv_ref, entering_ref, inner_ref, sent, landed, send_sem, recv_sem
):
    me = lax.axis_index("ctx")
    first, later = scan_shifts(count)
    partners = sorted(set(first + later))
    share = ending_ref.shape[1] // parts

    barrier = pltpu.get_barrier_semaphore()
    for span in partners:
        for target in (lax.rem(me + span, count), lax.rem(me + count - span, count)):
            pl.semaphore_signal(barrier, inc=1, device_id={"ctx": target}, device_id_type=pl.DeviceIdType.MESH)
    pl.semaphore_wait(barrier, 2 * len(partners))

    started = []

    def send(source, slot, part, span):
        copy = pltpu.make_async_remote_copy(
            src_ref=source,
            dst_ref=landed.at[slot, part],
            send_sem=send_sem.at[slot, part],
            recv_sem=recv_sem.at[slot, part],
            device_id={"ctx": lax.rem(me + span, count)},
            device_id_type=pl.DeviceIdType.MESH,
        )

        @pl.when(me + span < count)
        def _():
            copy.start()

        started.append((copy, span))
        return (copy, slot, part, span)

    def take(copy, slot, part, span, factor):
        columns = pl.ds(part * share, share)

        @pl.when(me >= span)
        def _():
            copy.wait_recv()
            if factor is None:
                entering_ref[:, columns] += landed[slot, part]
            else:
                entering_ref[:, columns] += decay_ref[factor, :, columns] * landed[slot, part]

    tiles = kv_ref.shape[1] // 128
    rounds = 1 + len(later)
    bounds = [tiles * step // rounds for step in range(rounds + 1)]

    entering_ref[...] = jnp.zeros(entering_ref.shape, jnp.float32)
    pending = []
    for part in range(parts):
        columns = pl.ds(part * share, share)
        pending.append(
            [
                send(ending_ref.at[:, columns], slot, part, span) + (None if slot == 0 else 0,)
                for slot, span in enumerate(first)
            ]
        )
    conv_tiles(high_ref, low_ref, kv_ref, inner_ref, bounds[0], bounds[1])
    for step in range(len(later) + 1):
        for part in range(parts):
            for copy, slot, owner, span, factor in pending[part]:
                take(copy, slot, owner, span, factor)
            if step < len(later):
                slot = len(first) + step
                sent[step, part] = entering_ref[:, pl.ds(part * share, share)]
                pending[part] = [send(sent.at[step, part], slot, part, later[step]) + (step + 1,)]
        if step < len(later):
            conv_tiles(high_ref, low_ref, kv_ref, inner_ref, bounds[step + 1], bounds[step + 2])
    for copy, span in started:

        @pl.when(me + span < count)
        def _():
            copy.wait_send()


def scan_states(ending, decay, high, low, kv, parts=2):
    count = lax.axis_size("ctx")
    first, later = scan_shifts(count)
    slots = len(first) + len(later)
    share = (ending.shape[0], ending.shape[1] // parts)
    vmem = pl.BlockSpec(memory_space=pltpu.VMEM)
    return pl.pallas_call(
        functools.partial(scan_kernel, count, parts),
        out_shape=(
            jax.ShapeDtypeStruct(ending.shape, jnp.float32),
            jax.ShapeDtypeStruct(kv.shape, jnp.float32),
        ),
        in_specs=[vmem] * 5,
        out_specs=(vmem, vmem),
        scratch_shapes=[
            pltpu.VMEM((max(1, len(later)), parts) + share, jnp.float32),
            pltpu.VMEM((slots, parts) + share, jnp.float32),
            pltpu.SemaphoreType.DMA((slots, parts)),
            pltpu.SemaphoreType.DMA((slots, parts)),
        ],
        compiler_params=pltpu.CompilerParams(
            collective_id=0, has_side_effects=True, vmem_limit_bytes=48 * 1024 * 1024
        ),
    )(ending, decay, high, low, kv)


def local(query_in, key_in, value_in, feature_taps, decay_rate, residues, skip_gain, out_weight):
    pair = [(0, 1), (1, 0)]
    chip = lax.axis_index("zlo")
    core = lax.axis_index("core")
    cores = lax.axis_size("core")
    other_chip = (1 - chip) * cores
    remote = lax.ppermute(out_weight, "zlo", pair)
    weight_blocks = [
        (chip * cores + core, out_weight),
        (chip * cores + 1 - core, lax.ppermute(out_weight, "core", pair)),
        (other_chip + core, remote),
    ]
    query_rows = query_in[0]
    key_rows = key_in[0]
    value_rows = value_in[0]
    rows_here, chans = query_rows.shape
    keep = FEAT - 1
    tails = shifted(
        jnp.concatenate(
            [query_rows[rows_here - keep :], key_rows[rows_here - keep :], value_rows[rows_here - keep :]],
            axis=0,
        ),
        "ctx",
        1,
    )
    featured_q = featurize(query_rows, tails[0:keep], feature_taps[0])
    featured_k = featurize(key_rows, tails[keep : 2 * keep], feature_taps[1])
    featured_v = featurize(value_rows, tails[2 * keep :], feature_taps[2])
    kv_round = (featured_k * featured_v).astype(jnp.bfloat16)

    groups = chans // GROUP
    width = rows_here
    kv_grouped = kv_round.reshape(width, groups, GROUP)

    positions = jnp.arange(width, dtype=jnp.float32)
    scale = residues * jnp.sqrt(-jnp.expm1(-2.0 * decay_rate))
    powers = jnp.exp(-decay_rate[:, :, None] * positions)
    kernel = jnp.einsum("gm,gmt->gt", scale, powers, precision=exact_precision)
    closing = jnp.exp(-decay_rate[:, :, None] * (width - 1.0 - positions))
    lagged = jnp.exp(-decay_rate[:, :, None] * (positions + 1.0)) * scale[:, :, None]

    taps = jnp.roll(kernel[:, ::-1], 1, axis=1)
    high = lax.reduce_precision(taps, exponent_bits=8, mantissa_bits=7)
    low = lax.reduce_precision(taps - high, exponent_bits=8, mantissa_bits=7)
    ending = two_pass("gnj,jgc->ngc", closing, kv_grouped).reshape(-1, chans)

    first, later = scan_shifts(lax.axis_size("ctx"))
    spans = jnp.asarray([1] * (len(first) - 1) + later, jnp.float32)[:, None, None] * float(width)
    modes = decay_rate.shape[1]
    rate_lanes = jnp.broadcast_to(jnp.transpose(decay_rate)[:, :, None], (modes, groups, GROUP))
    decay = jnp.exp(-rate_lanes.reshape(1, modes, chans) * spans)
    entering, inner = scan_states(ending, decay, high, low, kv_round)
    entering, remote = lax.optimization_barrier((entering, remote))
    weight_blocks.append((other_chip + 1 - core, lax.ppermute(remote, "core", [(0, 1), (1, 0)])))
    entering = entering.reshape(-1, groups, GROUP)
    crossing = jnp.einsum("gni,ngc->igc", lagged, entering, precision=exact_precision)
    convolved = (inner + crossing.reshape(width, chans)).astype(jnp.bfloat16)

    gated = (
        featured_q * (convolved.astype(jnp.float32) + skip_gain * kv_round.astype(jnp.float32))
    ).astype(jnp.bfloat16)
    rows = out_weight.shape[0]
    block_out = None
    for owner, weight in weight_blocks:
        columns = lax.dynamic_slice_in_dim(gated, owner * rows, rows, axis=1)
        term = jnp.dot(columns, weight, preferred_element_type=jnp.float32)
        block_out = term if block_out is None else block_out + term
    return block_out.astype(jnp.bfloat16)[None]


def solution(mesh):
    ctx_size, fsdp_size = mesh.shape["ctx"], mesh.shape["fsdp"]
    split = jax.sharding.Mesh(
        mesh.devices.reshape(ctx_size, fsdp_size // 2, 2), ("ctx", "zlo", "core")
    )
    batch = ("zlo", "core")
    return jax.shard_map(
        local,
        mesh=split,
        in_specs=(
            P(batch, "ctx", None),
            P(batch, "ctx", None),
            P(batch, "ctx", None),
            P(),
            P(),
            P(),
            P(),
            P(batch, None),
        ),
        out_specs=P(batch, "ctx", None),
        check_vma=False,
    )
```

```python
import functools

import jax
import jax.numpy as jnp
from jax import lax
from jax.experimental import pallas as pl
from jax.experimental.pallas import tpu as pltpu
from jax.sharding import PartitionSpec as P

GROUP = 16
FEAT = 3

exact_precision = lax.Precision.HIGHEST


def shifted(shard, axis, by):
    count = lax.axis_size(axis)
    pairs = [(i, i + by) for i in range(count) if 0 <= i + by < count]
    return lax.ppermute(shard, axis, pairs)


def featurize(rows, tail, taps_one):
    values = jnp.concatenate([tail, rows], axis=0).astype(jnp.float32)
    count = rows.shape[0]
    total = taps_one[0] * values[FEAT - 1 :]
    for offset in range(1, FEAT):
        total = total + taps_one[offset] * values[FEAT - 1 - offset : FEAT - 1 - offset + count]
    return total


def split_bf16(values):
    rounded = lax.reduce_precision(values, exponent_bits=8, mantissa_bits=7)
    return rounded.astype(jnp.bfloat16), (values - rounded).astype(jnp.bfloat16)


def two_pass(spec, table, signal):
    high, low = split_bf16(table)
    first = jnp.einsum(spec, high, signal, preferred_element_type=jnp.float32)
    return first + jnp.einsum(spec, low, signal, preferred_element_type=jnp.float32)


def scan_shifts(count):
    first = [1, 2] if count > 2 else [1]
    later = []
    span = 2
    while span < count:
        later.append(span)
        span *= 2
    return first, later


def conv_tiles(high_ref, low_ref, kv_ref, inner_ref, first_tile, last_tile):
    width = kv_ref.shape[0]
    per_tile = 128 // GROUP
    owner = lax.broadcasted_iota(jnp.int32, (1, 128), 1) // GROUP
    causal = lax.broadcasted_iota(jnp.int32, (width, width), 1) <= lax.broadcasted_iota(
        jnp.int32, (width, width), 0
    )

    def toeplitz_part(ref, group):
        row = ref[pl.ds(group, 1), :]
        rolled = pltpu.roll(jnp.broadcast_to(row, (width, width)), 0, 1, stride=1, stride_axis=0)
        return jnp.where(causal, rolled, 0.0).astype(jnp.bfloat16)

    def body(tile, carry):
        col = pl.multiple_of(tile * 128, 128)
        block = kv_ref[:, pl.ds(col, 128)]
        total = jnp.zeros((width, 128), jnp.float32)
        for member in range(per_tile):
            group = tile * per_tile + member
            part = jnp.where(owner == member, block, jnp.zeros_like(block))
            total += jnp.dot(toeplitz_part(high_ref, group), part, preferred_element_type=jnp.float32)
            total += jnp.dot(toeplitz_part(low_ref, group), part, preferred_element_type=jnp.float32)
        inner_ref[:, pl.ds(col, 128)] = total
        return carry

    lax.fori_loop(first_tile, last_tile, body, 0)


def scan_kernel(
    count,
    parts,
    ending_ref,
    decay_ref,
    high_ref,
    low_ref,
    kv_ref,
    weight_ref,
    entering_ref,
    inner_ref,
    blocks_ref,
    sent,
    landed,
    send_sem,
    recv_sem,
    weight_send,
    weight_recv,
):
    me = lax.axis_index("ctx")
    first, later = scan_shifts(count)
    partners = sorted(set(first + later))
    share = ending_ref.shape[1] // parts
    core_partner = {"core": 1 - lax.axis_index("core")}
    chip_partner = {"zlo": 1 - lax.axis_index("zlo")}

    barrier = pltpu.get_barrier_semaphore()
    for span in partners:
        for target in (lax.rem(me + span, count), lax.rem(me + count - span, count)):
            pl.semaphore_signal(barrier, inc=1, device_id={"ctx": target}, device_id_type=pl.DeviceIdType.MESH)
    for partner in (core_partner, chip_partner):
        pl.semaphore_signal(barrier, inc=1, device_id=partner, device_id_type=pl.DeviceIdType.MESH)
    pl.semaphore_wait(barrier, 2 * len(partners) + 2)

    def weight_copy(source, slot, partner):
        copy = pltpu.make_async_remote_copy(
            src_ref=source,
            dst_ref=blocks_ref.at[slot],
            send_sem=weight_send.at[slot],
            recv_sem=weight_recv.at[slot],
            device_id=partner,
            device_id_type=pl.DeviceIdType.MESH,
        )
        copy.start()
        return copy

    weight_copies = [weight_copy(weight_ref, 0, core_partner), weight_copy(weight_ref, 1, chip_partner)]

    started = []

    def send(source, slot, part, span):
        copy = pltpu.make_async_remote_copy(
            src_ref=source,
            dst_ref=landed.at[slot, part],
            send_sem=send_sem.at[slot, part],
            recv_sem=recv_sem.at[slot, part],
            device_id={"ctx": lax.rem(me + span, count)},
            device_id_type=pl.DeviceIdType.MESH,
        )

        @pl.when(me + span < count)
        def _():
            copy.start()

        started.append((copy, span))
        return (copy, slot, part, span)

    def take(copy, slot, part, span, factor):
        columns = pl.ds(part * share, share)

        @pl.when(me >= span)
        def _():
            copy.wait_recv()
            if factor is None:
                entering_ref[:, columns] += landed[slot, part]
            else:
                entering_ref[:, columns] += decay_ref[factor, :, columns] * landed[slot, part]

    tiles = kv_ref.shape[1] // 128
    rounds = 1 + len(later)
    bounds = [tiles * step // rounds for step in range(rounds + 1)]

    entering_ref[...] = jnp.zeros(entering_ref.shape, jnp.float32)
    pending = []
    for part in range(parts):
        columns = pl.ds(part * share, share)
        pending.append(
            [
                send(ending_ref.at[:, columns], slot, part, span) + (None if slot == 0 else 0,)
                for slot, span in enumerate(first)
            ]
        )
    conv_tiles(high_ref, low_ref, kv_ref, inner_ref, bounds[0], bounds[1])
    for step in range(len(later) + 1):
        for part in range(parts):
            for copy, slot, owner, span, factor in pending[part]:
                take(copy, slot, owner, span, factor)
            if step < len(later):
                slot = len(first) + step
                sent[step, part] = entering_ref[:, pl.ds(part * share, share)]
                pending[part] = [send(sent.at[step, part], slot, part, later[step]) + (step + 1,)]
        if step == len(later) - 1:
            weight_copies[1].wait_recv()
            weight_copies.append(weight_copy(blocks_ref.at[1], 2, core_partner))
        if step < len(later):
            conv_tiles(high_ref, low_ref, kv_ref, inner_ref, bounds[step + 1], bounds[step + 2])
    for copy in weight_copies:
        copy.wait_send()
    weight_copies[0].wait_recv()
    weight_copies[2].wait_recv()
    for copy, span in started:

        @pl.when(me + span < count)
        def _():
            copy.wait_send()


def scan_states(ending, decay, high, low, kv, weight, parts=2):
    count = lax.axis_size("ctx")
    first, later = scan_shifts(count)
    slots = len(first) + len(later)
    share = (ending.shape[0], ending.shape[1] // parts)
    vmem = pl.BlockSpec(memory_space=pltpu.VMEM)
    anywhere = pl.BlockSpec(memory_space=pl.ANY)
    return pl.pallas_call(
        functools.partial(scan_kernel, count, parts),
        out_shape=(
            jax.ShapeDtypeStruct(ending.shape, jnp.float32),
            jax.ShapeDtypeStruct(kv.shape, jnp.float32),
            jax.ShapeDtypeStruct((3,) + weight.shape, weight.dtype),
        ),
        in_specs=[vmem] * 5 + [anywhere],
        out_specs=(vmem, vmem, anywhere),
        scratch_shapes=[
            pltpu.VMEM((max(1, len(later)), parts) + share, jnp.float32),
            pltpu.VMEM((slots, parts) + share, jnp.float32),
            pltpu.SemaphoreType.DMA((slots, parts)),
            pltpu.SemaphoreType.DMA((slots, parts)),
            pltpu.SemaphoreType.DMA((3,)),
            pltpu.SemaphoreType.DMA((3,)),
        ],
        compiler_params=pltpu.CompilerParams(
            collective_id=0, has_side_effects=True, vmem_limit_bytes=48 * 1024 * 1024
        ),
    )(ending, decay, high, low, kv, weight)


def local(query_in, key_in, value_in, feature_taps, decay_rate, residues, skip_gain, out_weight):
    query_rows = query_in[0]
    key_rows = key_in[0]
    value_rows = value_in[0]
    rows_here, chans = query_rows.shape
    keep = FEAT - 1
    tails = shifted(
        jnp.concatenate(
            [query_rows[rows_here - keep :], key_rows[rows_here - keep :], value_rows[rows_here - keep :]],
            axis=0,
        ),
        "ctx",
        1,
    )
    featured_q = featurize(query_rows, tails[0:keep], feature_taps[0])
    featured_k = featurize(key_rows, tails[keep : 2 * keep], feature_taps[1])
    featured_v = featurize(value_rows, tails[2 * keep :], feature_taps[2])
    kv_round = (featured_k * featured_v).astype(jnp.bfloat16)

    groups = chans // GROUP
    width = rows_here
    kv_grouped = kv_round.reshape(width, groups, GROUP)

    positions = jnp.arange(width, dtype=jnp.float32)
    scale = residues * jnp.sqrt(-jnp.expm1(-2.0 * decay_rate))
    powers = jnp.exp(-decay_rate[:, :, None] * positions)
    kernel = jnp.einsum("gm,gmt->gt", scale, powers, precision=exact_precision)
    closing = jnp.exp(-decay_rate[:, :, None] * (width - 1.0 - positions))
    lagged = jnp.exp(-decay_rate[:, :, None] * (positions + 1.0)) * scale[:, :, None]

    taps = jnp.roll(kernel[:, ::-1], 1, axis=1)
    high = lax.reduce_precision(taps, exponent_bits=8, mantissa_bits=7)
    low = lax.reduce_precision(taps - high, exponent_bits=8, mantissa_bits=7)
    ending = two_pass("gnj,jgc->ngc", closing, kv_grouped).reshape(-1, chans)

    first, later = scan_shifts(lax.axis_size("ctx"))
    spans = jnp.asarray([1] * (len(first) - 1) + later, jnp.float32)[:, None, None] * float(width)
    modes = decay_rate.shape[1]
    rate_lanes = jnp.broadcast_to(jnp.transpose(decay_rate)[:, :, None], (modes, groups, GROUP))
    decay = jnp.exp(-rate_lanes.reshape(1, modes, chans) * spans)
    entering, inner, blocks = scan_states(ending, decay, high, low, kv_round, out_weight)
    chip = lax.axis_index("zlo")
    core = lax.axis_index("core")
    cores = lax.axis_size("core")
    other_chip = (1 - chip) * cores
    weight_blocks = [
        (chip * cores + core, out_weight),
        (chip * cores + 1 - core, blocks[0]),
        (other_chip + core, blocks[1]),
        (other_chip + 1 - core, blocks[2]),
    ]
    entering = entering.reshape(-1, groups, GROUP)
    crossing = jnp.einsum("gni,ngc->igc", lagged, entering, precision=exact_precision)
    convolved = (inner + crossing.reshape(width, chans)).astype(jnp.bfloat16)

    gated = (
        featured_q * (convolved.astype(jnp.float32) + skip_gain * kv_round.astype(jnp.float32))
    ).astype(jnp.bfloat16)
    rows = out_weight.shape[0]
    block_out = None
    for owner, weight in weight_blocks:
        columns = lax.dynamic_slice_in_dim(gated, owner * rows, rows, axis=1)
        term = jnp.dot(columns, weight, preferred_element_type=jnp.float32)
        block_out = term if block_out is None else block_out + term
    return block_out.astype(jnp.bfloat16)[None]


def solution(mesh):
    ctx_size, fsdp_size = mesh.shape["ctx"], mesh.shape["fsdp"]
    split = jax.sharding.Mesh(
        mesh.devices.reshape(ctx_size, fsdp_size // 2, 2), ("ctx", "zlo", "core")
    )
    batch = ("zlo", "core")
    return jax.shard_map(
        local,
        mesh=split,
        in_specs=(
            P(batch, "ctx", None),
            P(batch, "ctx", None),
            P(batch, "ctx", None),
            P(),
            P(),
            P(),
            P(),
            P(batch, None),
        ),
        out_specs=P(batch, "ctx", None),
        check_vma=False,
    )
```

```python
import functools

import jax
import jax.numpy as jnp
from jax import lax
from jax.experimental import pallas as pl
from jax.experimental.pallas import tpu as pltpu
from jax.sharding import PartitionSpec as P

GROUP = 16
FEAT = 3

exact_precision = lax.Precision.HIGHEST


def shifted(shard, axis, by):
    count = lax.axis_size(axis)
    pairs = [(i, i + by) for i in range(count) if 0 <= i + by < count]
    return lax.ppermute(shard, axis, pairs)


def featurize(rows, tail, taps_one):
    values = jnp.concatenate([tail, rows], axis=0).astype(jnp.float32)
    count = rows.shape[0]
    total = taps_one[0] * values[FEAT - 1 :]
    for offset in range(1, FEAT):
        total = total + taps_one[offset] * values[FEAT - 1 - offset : FEAT - 1 - offset + count]
    return total


def split_bf16(values):
    rounded = lax.reduce_precision(values, exponent_bits=8, mantissa_bits=7)
    return rounded.astype(jnp.bfloat16), (values - rounded).astype(jnp.bfloat16)


def two_pass(spec, table, signal):
    high, low = split_bf16(table)
    first = jnp.einsum(spec, high, signal, preferred_element_type=jnp.float32)
    return first + jnp.einsum(spec, low, signal, preferred_element_type=jnp.float32)


def scan_shifts(count):
    first = [1, 2] if count > 2 else [1]
    later = []
    span = 2
    while span < count:
        later.append(span)
        span *= 2
    return first, later


def conv_tiles(high_ref, low_ref, kv_ref, inner_ref, first_tile, last_tile):
    width = kv_ref.shape[0]
    per_tile = 128 // GROUP
    owner = lax.broadcasted_iota(jnp.int32, (1, 128), 1) // GROUP
    causal = lax.broadcasted_iota(jnp.int32, (width, width), 1) <= lax.broadcasted_iota(
        jnp.int32, (width, width), 0
    )

    def toeplitz_part(ref, group):
        row = ref[pl.ds(group, 1), :]
        rolled = pltpu.roll(jnp.broadcast_to(row, (width, width)), 0, 1, stride=1, stride_axis=0)
        return jnp.where(causal, rolled, 0.0).astype(jnp.bfloat16)

    def body(tile, carry):
        col = pl.multiple_of(tile * 128, 128)
        block = kv_ref[:, pl.ds(col, 128)]
        total = jnp.zeros((width, 128), jnp.float32)
        for member in range(per_tile):
            group = tile * per_tile + member
            part = jnp.where(owner == member, block, jnp.zeros_like(block))
            total += jnp.dot(toeplitz_part(high_ref, group), part, preferred_element_type=jnp.float32)
            total += jnp.dot(toeplitz_part(low_ref, group), part, preferred_element_type=jnp.float32)
        inner_ref[:, pl.ds(col, 128)] = total
        return carry

    lax.fori_loop(first_tile, last_tile, body, 0)


def scan_kernel(
    count, parts, ending_ref, decay_ref, high_ref, low_ref, kv_ref, entering_ref, inner_ref, sent, landed, send_sem, recv_sem
):
    me = lax.axis_index("ctx")
    first, later = scan_shifts(count)
    partners = sorted(set(first + later))
    share = ending_ref.shape[1] // parts

    barrier = pltpu.get_barrier_semaphore()
    for span in partners:
        for target in (lax.rem(me + span, count), lax.rem(me + count - span, count)):
            pl.semaphore_signal(barrier, inc=1, device_id={"ctx": target}, device_id_type=pl.DeviceIdType.MESH)
    pl.semaphore_wait(barrier, 2 * len(partners))

    started = []

    def send(source, slot, part, span):
        copy = pltpu.make_async_remote_copy(
            src_ref=source,
            dst_ref=landed.at[slot, part],
            send_sem=send_sem.at[slot, part],
            recv_sem=recv_sem.at[slot, part],
            device_id={"ctx": lax.rem(me + span, count)},
            device_id_type=pl.DeviceIdType.MESH,
        )

        @pl.when(me + span < count)
        def _():
            copy.start()

        started.append((copy, span))
        return (copy, slot, part, span)

    def take(copy, slot, part, span, factor):
        columns = pl.ds(part * share, share)

        @pl.when(me >= span)
        def _():
            copy.wait_recv()
            if factor is None:
                entering_ref[:, columns] += landed[slot, part]
            else:
                entering_ref[:, columns] += decay_ref[factor, :, columns] * landed[slot, part]

    tiles = kv_ref.shape[1] // 128
    rounds = 1 + len(later)
    bounds = [tiles * step // rounds for step in range(rounds + 1)]

    entering_ref[...] = jnp.zeros(entering_ref.shape, jnp.float32)
    pending = []
    for part in range(parts):
        columns = pl.ds(part * share, share)
        pending.append(
            [
                send(ending_ref.at[:, columns], slot, part, span) + (None if slot == 0 else 0,)
                for slot, span in enumerate(first)
            ]
        )
    conv_tiles(high_ref, low_ref, kv_ref, inner_ref, bounds[0], bounds[1])
    for step in range(len(later) + 1):
        for part in range(parts):
            for copy, slot, owner, span, factor in pending[part]:
                take(copy, slot, owner, span, factor)
            if step < len(later):
                slot = len(first) + step
                sent[step, part] = entering_ref[:, pl.ds(part * share, share)]
                pending[part] = [send(sent.at[step, part], slot, part, later[step]) + (step + 1,)]
        if step < len(later):
            conv_tiles(high_ref, low_ref, kv_ref, inner_ref, bounds[step + 1], bounds[step + 2])
    for copy, span in started:

        @pl.when(me + span < count)
        def _():
            copy.wait_send()


def scan_states(ending, decay, high, low, kv, parts=4):
    count = lax.axis_size("ctx")
    first, later = scan_shifts(count)
    slots = len(first) + len(later)
    share = (ending.shape[0], ending.shape[1] // parts)
    vmem = pl.BlockSpec(memory_space=pltpu.VMEM)
    return pl.pallas_call(
        functools.partial(scan_kernel, count, parts),
        out_shape=(
            jax.ShapeDtypeStruct(ending.shape, jnp.float32),
            jax.ShapeDtypeStruct(kv.shape, jnp.float32),
        ),
        in_specs=[vmem] * 5,
        out_specs=(vmem, vmem),
        scratch_shapes=[
            pltpu.VMEM((max(1, len(later)), parts) + share, jnp.float32),
            pltpu.VMEM((slots, parts) + share, jnp.float32),
            pltpu.SemaphoreType.DMA((slots, parts)),
            pltpu.SemaphoreType.DMA((slots, parts)),
        ],
        compiler_params=pltpu.CompilerParams(
            collective_id=0, has_side_effects=True, vmem_limit_bytes=48 * 1024 * 1024
        ),
    )(ending, decay, high, low, kv)


def local(query_in, key_in, value_in, feature_taps, decay_rate, residues, skip_gain, out_weight):
    pair = [(0, 1), (1, 0)]
    chip = lax.axis_index("zlo")
    core = lax.axis_index("core")
    cores = lax.axis_size("core")
    other_chip = (1 - chip) * cores
    remote = lax.ppermute(out_weight, "zlo", pair)
    weight_blocks = [
        (chip * cores + core, out_weight),
        (chip * cores + 1 - core, lax.ppermute(out_weight, "core", pair)),
        (other_chip + core, remote),
    ]
    query_rows = query_in[0]
    key_rows = key_in[0]
    value_rows = value_in[0]
    rows_here, chans = query_rows.shape
    keep = FEAT - 1
    tails = shifted(
        jnp.concatenate(
            [query_rows[rows_here - keep :], key_rows[rows_here - keep :], value_rows[rows_here - keep :]],
            axis=0,
        ),
        "ctx",
        1,
    )
    featured_q = featurize(query_rows, tails[0:keep], feature_taps[0])
    featured_k = featurize(key_rows, tails[keep : 2 * keep], feature_taps[1])
    featured_v = featurize(value_rows, tails[2 * keep :], feature_taps[2])
    kv_round = (featured_k * featured_v).astype(jnp.bfloat16)

    groups = chans // GROUP
    width = rows_here
    kv_grouped = kv_round.reshape(width, groups, GROUP)

    positions = jnp.arange(width, dtype=jnp.float32)
    scale = residues * jnp.sqrt(-jnp.expm1(-2.0 * decay_rate))
    powers = jnp.exp(-decay_rate[:, :, None] * positions)
    kernel = jnp.einsum("gm,gmt->gt", scale, powers, precision=exact_precision)
    closing = jnp.exp(-decay_rate[:, :, None] * (width - 1.0 - positions))
    lagged = jnp.exp(-decay_rate[:, :, None] * (positions + 1.0)) * scale[:, :, None]

    taps = jnp.roll(kernel[:, ::-1], 1, axis=1)
    high = lax.reduce_precision(taps, exponent_bits=8, mantissa_bits=7)
    low = lax.reduce_precision(taps - high, exponent_bits=8, mantissa_bits=7)
    ending = two_pass("gnj,jgc->ngc", closing, kv_grouped).reshape(-1, chans)

    first, later = scan_shifts(lax.axis_size("ctx"))
    spans = jnp.asarray([1] * (len(first) - 1) + later, jnp.float32)[:, None, None] * float(width)
    modes = decay_rate.shape[1]
    rate_lanes = jnp.broadcast_to(jnp.transpose(decay_rate)[:, :, None], (modes, groups, GROUP))
    decay = jnp.exp(-rate_lanes.reshape(1, modes, chans) * spans)
    entering, inner = scan_states(ending, decay, high, low, kv_round)
    entering, remote = lax.optimization_barrier((entering, remote))
    weight_blocks.append((other_chip + 1 - core, lax.ppermute(remote, "core", [(0, 1), (1, 0)])))
    entering = entering.reshape(-1, groups, GROUP)
    crossing = jnp.einsum("gni,ngc->igc", lagged, entering, precision=exact_precision)
    convolved = (inner + crossing.reshape(width, chans)).astype(jnp.bfloat16)

    gated = (
        featured_q * (convolved.astype(jnp.float32) + skip_gain * kv_round.astype(jnp.float32))
    ).astype(jnp.bfloat16)
    rows = out_weight.shape[0]
    block_out = None
    for owner, weight in weight_blocks:
        columns = lax.dynamic_slice_in_dim(gated, owner * rows, rows, axis=1)
        term = jnp.dot(columns, weight, preferred_element_type=jnp.float32)
        block_out = term if block_out is None else block_out + term
    return block_out.astype(jnp.bfloat16)[None]


def solution(mesh):
    ctx_size, fsdp_size = mesh.shape["ctx"], mesh.shape["fsdp"]
    split = jax.sharding.Mesh(
        mesh.devices.reshape(ctx_size, fsdp_size // 2, 2), ("ctx", "zlo", "core")
    )
    batch = ("zlo", "core")
    return jax.shard_map(
        local,
        mesh=split,
        in_specs=(
            P(batch, "ctx", None),
            P(batch, "ctx", None),
            P(batch, "ctx", None),
            P(),
            P(),
            P(),
            P(),
            P(batch, None),
        ),
        out_specs=P(batch, "ctx", None),
        check_vma=False,
    )
```

```python
import functools

import jax
import jax.numpy as jnp
from jax import lax
from jax.experimental import pallas as pl
from jax.experimental.pallas import tpu as pltpu
from jax.sharding import PartitionSpec as P

GROUP = 16
FEAT = 3

exact_precision = lax.Precision.HIGHEST


def shifted(shard, axis, by):
    count = lax.axis_size(axis)
    pairs = [(i, i + by) for i in range(count) if 0 <= i + by < count]
    return lax.ppermute(shard, axis, pairs)


def featurize(rows, tail, taps_one):
    values = jnp.concatenate([tail, rows], axis=0).astype(jnp.float32)
    count = rows.shape[0]
    total = taps_one[0] * values[FEAT - 1 :]
    for offset in range(1, FEAT):
        total = total + taps_one[offset] * values[FEAT - 1 - offset : FEAT - 1 - offset + count]
    return total


def split_bf16(values):
    rounded = lax.reduce_precision(values, exponent_bits=8, mantissa_bits=7)
    return rounded.astype(jnp.bfloat16), (values - rounded).astype(jnp.bfloat16)


def two_pass(spec, table, signal):
    high, low = split_bf16(table)
    first = jnp.einsum(spec, high, signal, preferred_element_type=jnp.float32)
    return first + jnp.einsum(spec, low, signal, preferred_element_type=jnp.float32)


def scan_shifts(count):
    first = [1, 2] if count > 2 else [1]
    later = []
    span = 2
    while span < count:
        later.append(span)
        span *= 2
    return first, later


def conv_tiles(high_ref, low_ref, kv_ref, inner_ref, first_tile, last_tile):
    width = kv_ref.shape[0]
    per_tile = 128 // GROUP
    owner = lax.broadcasted_iota(jnp.int32, (1, 128), 1) // GROUP
    causal = lax.broadcasted_iota(jnp.int32, (width, width), 1) <= lax.broadcasted_iota(
        jnp.int32, (width, width), 0
    )

    def toeplitz_part(ref, group):
        row = ref[pl.ds(group, 1), :]
        rolled = pltpu.roll(jnp.broadcast_to(row, (width, width)), 0, 1, stride=1, stride_axis=0)
        return jnp.where(causal, rolled, 0.0).astype(jnp.bfloat16)

    def body(tile, carry):
        col = pl.multiple_of(tile * 128, 128)
        block = kv_ref[:, pl.ds(col, 128)]
        total = jnp.zeros((width, 128), jnp.float32)
        for member in range(per_tile):
            group = tile * per_tile + member
            part = jnp.where(owner == member, block, jnp.zeros_like(block))
            total += jnp.dot(toeplitz_part(high_ref, group), part, preferred_element_type=jnp.float32)
            total += jnp.dot(toeplitz_part(low_ref, group), part, preferred_element_type=jnp.float32)
        inner_ref[:, pl.ds(col, 128)] = total
        return carry

    lax.fori_loop(first_tile, last_tile, body, 0)


def scan_kernel(
    count, parts, ending_ref, decay_ref, high_ref, low_ref, kv_ref, entering_ref, inner_ref, sent, landed, send_sem, recv_sem
):
    me = lax.axis_index("ctx")
    first, later = scan_shifts(count)
    partners = sorted(set(first + later))
    share = ending_ref.shape[1] // parts

    barrier = pltpu.get_barrier_semaphore()
    for span in partners:
        for target in (lax.rem(me + span, count), lax.rem(me + count - span, count)):
            pl.semaphore_signal(barrier, inc=1, device_id={"ctx": target}, device_id_type=pl.DeviceIdType.MESH)
    pl.semaphore_wait(barrier, 2 * len(partners))

    started = []

    def send(source, slot, part, span):
        copy = pltpu.make_async_remote_copy(
            src_ref=source,
            dst_ref=landed.at[slot, part],
            send_sem=send_sem.at[slot, part],
            recv_sem=recv_sem.at[slot, part],
            device_id={"ctx": lax.rem(me + span, count)},
            device_id_type=pl.DeviceIdType.MESH,
        )

        @pl.when(me + span < count)
        def _():
            copy.start()

        started.append((copy, span))
        return (copy, slot, part, span)

    def take(copy, slot, part, span, factor):
        columns = pl.ds(part * share, share)

        @pl.when(me >= span)
        def _():
            copy.wait_recv()
            if factor is None:
                entering_ref[:, columns] += landed[slot, part]
            else:
                entering_ref[:, columns] += decay_ref[factor, :, columns] * landed[slot, part]

    tiles = kv_ref.shape[1] // 128
    rounds = 1 + len(later)
    bounds = [tiles * step // rounds for step in range(rounds + 1)]

    entering_ref[...] = jnp.zeros(entering_ref.shape, jnp.float32)
    pending = []
    for part in range(parts):
        columns = pl.ds(part * share, share)
        pending.append(
            [
                send(ending_ref.at[:, columns], slot, part, span) + (None if slot == 0 else 0,)
                for slot, span in enumerate(first)
            ]
        )
    conv_tiles(high_ref, low_ref, kv_ref, inner_ref, bounds[0], bounds[1])
    for step in range(len(later) + 1):
        for part in range(parts):
            for copy, slot, owner, span, factor in pending[part]:
                take(copy, slot, owner, span, factor)
            if step < len(later):
                slot = len(first) + step
                sent[step, part] = entering_ref[:, pl.ds(part * share, share)]
                pending[part] = [send(sent.at[step, part], slot, part, later[step]) + (step + 1,)]
        if step < len(later):
            conv_tiles(high_ref, low_ref, kv_ref, inner_ref, bounds[step + 1], bounds[step + 2])
    for copy, span in started:

        @pl.when(me + span < count)
        def _():
            copy.wait_send()


def scan_states(ending, decay, high, low, kv, parts=4):
    count = lax.axis_size("ctx")
    first, later = scan_shifts(count)
    slots = len(first) + len(later)
    share = (ending.shape[0], ending.shape[1] // parts)
    vmem = pl.BlockSpec(memory_space=pltpu.VMEM)
    return pl.pallas_call(
        functools.partial(scan_kernel, count, parts),
        out_shape=(
            jax.ShapeDtypeStruct(ending.shape, jnp.float32),
            jax.ShapeDtypeStruct(kv.shape, jnp.float32),
        ),
        in_specs=[vmem] * 5,
        out_specs=(vmem, vmem),
        scratch_shapes=[
            pltpu.VMEM((max(1, len(later)), parts) + share, jnp.float32),
            pltpu.VMEM((slots, parts) + share, jnp.float32),
            pltpu.SemaphoreType.DMA((slots, parts)),
            pltpu.SemaphoreType.DMA((slots, parts)),
        ],
        compiler_params=pltpu.CompilerParams(
            collective_id=0, has_side_effects=True, vmem_limit_bytes=48 * 1024 * 1024
        ),
    )(ending, decay, high, low, kv)


def local(query_in, key_in, value_in, feature_taps, decay_rate, residues, skip_gain, out_weight):
    pair = [(0, 1), (1, 0)]
    chip = lax.axis_index("zlo")
    core = lax.axis_index("core")
    cores = lax.axis_size("core")
    other_chip = (1 - chip) * cores
    remote = lax.ppermute(out_weight, "zlo", pair)
    weight_blocks = [
        (chip * cores + core, out_weight),
        (chip * cores + 1 - core, lax.ppermute(out_weight, "core", pair)),
        (other_chip + core, remote),
    ]
    query_rows = query_in[0]
    key_rows = key_in[0]
    value_rows = value_in[0]
    rows_here, chans = query_rows.shape
    keep = FEAT - 1
    tails = shifted(
        jnp.concatenate(
            [query_rows[rows_here - keep :], key_rows[rows_here - keep :], value_rows[rows_here - keep :]],
            axis=0,
        ),
        "ctx",
        1,
    )
    featured_q = featurize(query_rows, tails[0:keep], feature_taps[0])
    featured_k = featurize(key_rows, tails[keep : 2 * keep], feature_taps[1])
    featured_v = featurize(value_rows, tails[2 * keep :], feature_taps[2])
    kv_round = lax.optimization_barrier((featured_k * featured_v).astype(jnp.bfloat16))

    groups = chans // GROUP
    width = rows_here
    kv_grouped = kv_round.reshape(width, groups, GROUP)

    positions = jnp.arange(width, dtype=jnp.float32)
    scale = residues * jnp.sqrt(-jnp.expm1(-2.0 * decay_rate))
    powers = jnp.exp(-decay_rate[:, :, None] * positions)
    kernel = jnp.einsum("gm,gmt->gt", scale, powers, precision=exact_precision)
    closing = jnp.exp(-decay_rate[:, :, None] * (width - 1.0 - positions))

    taps = jnp.roll(kernel[:, ::-1], 1, axis=1)
    high = lax.reduce_precision(taps, exponent_bits=8, mantissa_bits=7)
    low = lax.reduce_precision(taps - high, exponent_bits=8, mantissa_bits=7)
    ending = two_pass("gnj,jgc->ngc", closing, kv_grouped).reshape(-1, chans)

    first, later = scan_shifts(lax.axis_size("ctx"))
    spans = jnp.asarray([1] * (len(first) - 1) + later, jnp.float32)[:, None, None] * float(width)
    modes = decay_rate.shape[1]
    rate_lanes = jnp.broadcast_to(jnp.transpose(decay_rate)[:, :, None], (modes, groups, GROUP))
    decay = jnp.exp(-rate_lanes.reshape(1, modes, chans) * spans)
    entering, inner = scan_states(ending, decay, high, low, kv_round)
    entering, remote = lax.optimization_barrier((entering, remote))
    weight_blocks.append((other_chip + 1 - core, lax.ppermute(remote, "core", [(0, 1), (1, 0)])))
    scale_lanes = jnp.broadcast_to(jnp.transpose(scale)[:, :, None], (modes, groups, GROUP)).reshape(modes, 1, chans)
    steps = (positions + 1.0)[None, :, None]
    crossing = jnp.sum(
        scale_lanes * jnp.exp(-rate_lanes.reshape(modes, 1, chans) * steps) * entering[:, None, :], axis=0
    )
    convolved = lax.optimization_barrier((inner + crossing).astype(jnp.bfloat16))

    gated = (
        featured_q * (convolved.astype(jnp.float32) + skip_gain * kv_round.astype(jnp.float32))
    ).astype(jnp.bfloat16)
    rows = out_weight.shape[0]
    block_out = None
    for owner, weight in weight_blocks:
        columns = lax.dynamic_slice_in_dim(gated, owner * rows, rows, axis=1)
        term = jnp.dot(columns, weight, preferred_element_type=jnp.float32)
        block_out = term if block_out is None else block_out + term
    return block_out.astype(jnp.bfloat16)[None]


def solution(mesh):
    ctx_size, fsdp_size = mesh.shape["ctx"], mesh.shape["fsdp"]
    split = jax.sharding.Mesh(
        mesh.devices.reshape(ctx_size, fsdp_size // 2, 2), ("ctx", "zlo", "core")
    )
    batch = ("zlo", "core")
    return jax.shard_map(
        local,
        mesh=split,
        in_specs=(
            P(batch, "ctx", None),
            P(batch, "ctx", None),
            P(batch, "ctx", None),
            P(),
            P(),
            P(),
            P(),
            P(batch, None),
        ),
        out_specs=P(batch, "ctx", None),
        check_vma=False,
    )
```

```python
import functools

import jax
import jax.numpy as jnp
from jax import lax
from jax.experimental import pallas as pl
from jax.experimental.pallas import tpu as pltpu
from jax.sharding import PartitionSpec as P

GROUP = 16
FEAT = 3

exact_precision = lax.Precision.HIGHEST


def shifted(shard, axis, by):
    count = lax.axis_size(axis)
    pairs = [(i, i + by) for i in range(count) if 0 <= i + by < count]
    return lax.ppermute(shard, axis, pairs)


def featurize(rows, tail, taps_one):
    values = jnp.concatenate([tail, rows], axis=0).astype(jnp.float32)
    count = rows.shape[0]
    total = taps_one[0] * values[FEAT - 1 :]
    for offset in range(1, FEAT):
        total = total + taps_one[offset] * values[FEAT - 1 - offset : FEAT - 1 - offset + count]
    return total


def split_bf16(values):
    rounded = lax.reduce_precision(values, exponent_bits=8, mantissa_bits=7)
    return rounded.astype(jnp.bfloat16), (values - rounded).astype(jnp.bfloat16)


def two_pass(spec, table, signal):
    high, low = split_bf16(table)
    first = jnp.einsum(spec, high, signal, preferred_element_type=jnp.float32)
    return first + jnp.einsum(spec, low, signal, preferred_element_type=jnp.float32)


def scan_shifts(count):
    first = [1, 2] if count > 2 else [1]
    later = []
    span = 2
    while span < count:
        later.append(span)
        span *= 2
    return first, later


def conv_tiles(high_ref, low_ref, kv_ref, inner_ref, first_tile, last_tile):
    width = kv_ref.shape[0]
    per_tile = 128 // GROUP
    owner = lax.broadcasted_iota(jnp.int32, (1, 128), 1) // GROUP
    causal = lax.broadcasted_iota(jnp.int32, (width, width), 1) <= lax.broadcasted_iota(
        jnp.int32, (width, width), 0
    )

    lag = lax.broadcasted_iota(jnp.int32, (1, width), 1)
    lag = jnp.where(lag == 0, 0, width - lag).astype(jnp.float32)

    def taps_row(group):
        row = jnp.zeros((1, width), jnp.float32)
        for mode in range(high_ref.shape[1]):
            row = row + low_ref[group, mode] * jnp.exp(-high_ref[group, mode] * lag)
        high = row.astype(jnp.bfloat16).astype(jnp.float32)
        return high, (row - high).astype(jnp.bfloat16).astype(jnp.float32)

    def toeplitz_part(row):
        rolled = pltpu.roll(jnp.broadcast_to(row, (width, width)), 0, 1, stride=1, stride_axis=0)
        return jnp.where(causal, rolled, 0.0).astype(jnp.bfloat16)

    def body(tile, carry):
        col = pl.multiple_of(tile * 128, 128)
        block = kv_ref[:, pl.ds(col, 128)]
        total = jnp.zeros((width, 128), jnp.float32)
        for member in range(per_tile):
            group = tile * per_tile + member
            part = jnp.where(owner == member, block, jnp.zeros_like(block))
            for row in taps_row(group):
                total += jnp.dot(toeplitz_part(row), part, preferred_element_type=jnp.float32)
        inner_ref[:, pl.ds(col, 128)] = total
        return carry

    lax.fori_loop(first_tile, last_tile, body, 0)


def scan_kernel(
    count, parts, ending_ref, decay_ref, high_ref, low_ref, kv_ref, entering_ref, inner_ref, sent, landed, send_sem, recv_sem
):
    me = lax.axis_index("ctx")
    first, later = scan_shifts(count)
    partners = sorted(set(first + later))
    share = ending_ref.shape[1] // parts

    barrier = pltpu.get_barrier_semaphore()
    for span in partners:
        for target in (lax.rem(me + span, count), lax.rem(me + count - span, count)):
            pl.semaphore_signal(barrier, inc=1, device_id={"ctx": target}, device_id_type=pl.DeviceIdType.MESH)
    pl.semaphore_wait(barrier, 2 * len(partners))

    started = []

    def send(source, slot, part, span):
        copy = pltpu.make_async_remote_copy(
            src_ref=source,
            dst_ref=landed.at[slot, part],
            send_sem=send_sem.at[slot, part],
            recv_sem=recv_sem.at[slot, part],
            device_id={"ctx": lax.rem(me + span, count)},
            device_id_type=pl.DeviceIdType.MESH,
        )

        @pl.when(me + span < count)
        def _():
            copy.start()

        started.append((copy, span))
        return (copy, slot, part, span)

    def take(copy, slot, part, span, factor):
        columns = pl.ds(part * share, share)

        @pl.when(me >= span)
        def _():
            copy.wait_recv()
            if factor is None:
                entering_ref[:, columns] += landed[slot, part]
            else:
                decay = jnp.exp(decay_ref[:, columns] * (-float(factor * kv_ref.shape[0])))
                entering_ref[:, columns] += decay * landed[slot, part]

    tiles = kv_ref.shape[1] // 128
    rounds = 1 + len(later)
    bounds = [tiles * step // rounds for step in range(rounds + 1)]

    entering_ref[...] = jnp.zeros(entering_ref.shape, jnp.float32)
    pending = []
    for part in range(parts):
        columns = pl.ds(part * share, share)
        pending.append(
            [
                send(ending_ref.at[:, columns], slot, part, span) + (None if slot == 0 else 1,)
                for slot, span in enumerate(first)
            ]
        )
    conv_tiles(high_ref, low_ref, kv_ref, inner_ref, bounds[0], bounds[1])
    for step in range(len(later) + 1):
        for part in range(parts):
            for copy, slot, owner, span, factor in pending[part]:
                take(copy, slot, owner, span, factor)
            if step < len(later):
                slot = len(first) + step
                sent[step, part] = entering_ref[:, pl.ds(part * share, share)]
                pending[part] = [send(sent.at[step, part], slot, part, later[step]) + (later[step],)]
        if step < len(later):
            conv_tiles(high_ref, low_ref, kv_ref, inner_ref, bounds[step + 1], bounds[step + 2])
    for copy, span in started:

        @pl.when(me + span < count)
        def _():
            copy.wait_send()


def scan_states(ending, decay, high, low, kv, parts=4):
    count = lax.axis_size("ctx")
    first, later = scan_shifts(count)
    slots = len(first) + len(later)
    share = (ending.shape[0], ending.shape[1] // parts)
    vmem = pl.BlockSpec(memory_space=pltpu.VMEM)
    smem = pl.BlockSpec(memory_space=pltpu.SMEM)
    return pl.pallas_call(
        functools.partial(scan_kernel, count, parts),
        out_shape=(
            jax.ShapeDtypeStruct(ending.shape, jnp.float32),
            jax.ShapeDtypeStruct(kv.shape, jnp.float32),
        ),
        in_specs=[vmem, vmem, smem, smem, vmem],
        out_specs=(vmem, vmem),
        scratch_shapes=[
            pltpu.VMEM((max(1, len(later)), parts) + share, jnp.float32),
            pltpu.VMEM((slots, parts) + share, jnp.float32),
            pltpu.SemaphoreType.DMA((slots, parts)),
            pltpu.SemaphoreType.DMA((slots, parts)),
        ],
        compiler_params=pltpu.CompilerParams(
            collective_id=0, has_side_effects=True, vmem_limit_bytes=48 * 1024 * 1024
        ),
    )(ending, decay, high, low, kv)


def local(query_in, key_in, value_in, feature_taps, decay_rate, residues, skip_gain, out_weight):
    pair = [(0, 1), (1, 0)]
    chip = lax.axis_index("zlo")
    core = lax.axis_index("core")
    cores = lax.axis_size("core")
    other_chip = (1 - chip) * cores
    remote = lax.ppermute(out_weight, "zlo", pair)
    weight_blocks = [
        (chip * cores + core, out_weight),
        (chip * cores + 1 - core, lax.ppermute(out_weight, "core", pair)),
        (other_chip + core, remote),
    ]
    query_rows = query_in[0]
    key_rows = key_in[0]
    value_rows = value_in[0]
    rows_here, chans = query_rows.shape
    keep = FEAT - 1
    tails = shifted(
        jnp.concatenate(
            [query_rows[rows_here - keep :], key_rows[rows_here - keep :], value_rows[rows_here - keep :]],
            axis=0,
        ),
        "ctx",
        1,
    )
    featured_q = featurize(query_rows, tails[0:keep], feature_taps[0])
    featured_k = featurize(key_rows, tails[keep : 2 * keep], feature_taps[1])
    featured_v = featurize(value_rows, tails[2 * keep :], feature_taps[2])
    kv_round = lax.optimization_barrier((featured_k * featured_v).astype(jnp.bfloat16))

    groups = chans // GROUP
    width = rows_here
    kv_grouped = kv_round.reshape(width, groups, GROUP)

    positions = jnp.arange(width, dtype=jnp.float32)
    scale = residues * jnp.sqrt(-jnp.expm1(-2.0 * decay_rate))
    closing = jnp.exp(-decay_rate[:, :, None] * (width - 1.0 - positions))

    ending = two_pass("gnj,jgc->ngc", closing, kv_grouped).reshape(-1, chans)

    modes = decay_rate.shape[1]
    rate_lanes = jnp.broadcast_to(jnp.transpose(decay_rate)[:, :, None], (modes, groups, GROUP))
    entering, inner = scan_states(ending, rate_lanes.reshape(modes, chans), decay_rate, scale, kv_round)
    entering, remote = lax.optimization_barrier((entering, remote))
    weight_blocks.append((other_chip + 1 - core, lax.ppermute(remote, "core", [(0, 1), (1, 0)])))
    scale_lanes = jnp.broadcast_to(jnp.transpose(scale)[:, :, None], (modes, groups, GROUP)).reshape(modes, 1, chans)
    steps = (positions + 1.0)[None, :, None]
    crossing = jnp.sum(
        scale_lanes * jnp.exp(-rate_lanes.reshape(modes, 1, chans) * steps) * entering[:, None, :], axis=0
    )
    convolved = lax.optimization_barrier((inner + crossing).astype(jnp.bfloat16))

    gated = (
        featured_q * (convolved.astype(jnp.float32) + skip_gain * kv_round.astype(jnp.float32))
    ).astype(jnp.bfloat16)
    rows = out_weight.shape[0]
    block_out = None
    for owner, weight in weight_blocks:
        columns = lax.dynamic_slice_in_dim(gated, owner * rows, rows, axis=1)
        term = jnp.dot(columns, weight, preferred_element_type=jnp.float32)
        block_out = term if block_out is None else block_out + term
    return block_out.astype(jnp.bfloat16)[None]


def solution(mesh):
    ctx_size, fsdp_size = mesh.shape["ctx"], mesh.shape["fsdp"]
    split = jax.sharding.Mesh(
        mesh.devices.reshape(ctx_size, fsdp_size // 2, 2), ("ctx", "zlo", "core")
    )
    batch = ("zlo", "core")
    return jax.shard_map(
        local,
        mesh=split,
        in_specs=(
            P(batch, "ctx", None),
            P(batch, "ctx", None),
            P(batch, "ctx", None),
            P(),
            P(),
            P(),
            P(),
            P(batch, None),
        ),
        out_specs=P(batch, "ctx", None),
        check_vma=False,
    )
```

```python
import functools

import jax
import jax.numpy as jnp
from jax import lax
from jax.experimental import pallas as pl
from jax.experimental.pallas import tpu as pltpu
from jax.sharding import PartitionSpec as P

GROUP = 16
FEAT = 3

exact_precision = lax.Precision.HIGHEST


def shifted(shard, axis, by):
    count = lax.axis_size(axis)
    pairs = [(i, i + by) for i in range(count) if 0 <= i + by < count]
    return lax.ppermute(shard, axis, pairs)


def featurize(rows, tail, taps_one):
    values = jnp.concatenate([tail, rows], axis=0).astype(jnp.float32)
    count = rows.shape[0]
    total = taps_one[0] * values[FEAT - 1 :]
    for offset in range(1, FEAT):
        total = total + taps_one[offset] * values[FEAT - 1 - offset : FEAT - 1 - offset + count]
    return total


def split_bf16(values):
    rounded = lax.reduce_precision(values, exponent_bits=8, mantissa_bits=7)
    return rounded.astype(jnp.bfloat16), (values - rounded).astype(jnp.bfloat16)


def two_pass(spec, table, signal):
    high, low = split_bf16(table)
    first = jnp.einsum(spec, high, signal, preferred_element_type=jnp.float32)
    return first + jnp.einsum(spec, low, signal, preferred_element_type=jnp.float32)


def scan_shifts(count):
    first = [1, 2] if count > 2 else [1]
    later = []
    span = 2
    while span < count:
        later.append(span)
        span *= 2
    return first, later


def conv_tiles(high_ref, low_ref, kv_ref, inner_ref, first_tile, last_tile):
    width = kv_ref.shape[0]
    per_tile = 128 // GROUP
    owner = lax.broadcasted_iota(jnp.int32, (1, 128), 1) // GROUP
    causal = lax.broadcasted_iota(jnp.int32, (width, width), 1) <= lax.broadcasted_iota(
        jnp.int32, (width, width), 0
    )

    def toeplitz_part(ref, group):
        row = ref[pl.ds(group, 1), :]
        rolled = pltpu.roll(jnp.broadcast_to(row, (width, width)), 0, 1, stride=1, stride_axis=0)
        return jnp.where(causal, rolled, 0.0).astype(jnp.bfloat16)

    def body(tile, carry):
        col = pl.multiple_of(tile * 128, 128)
        block = kv_ref[:, pl.ds(col, 128)]
        total = jnp.zeros((width, 128), jnp.float32)
        for member in range(per_tile):
            group = tile * per_tile + member
            part = jnp.where(owner == member, block, jnp.zeros_like(block))
            total += jnp.dot(toeplitz_part(high_ref, group), part, preferred_element_type=jnp.float32)
            total += jnp.dot(toeplitz_part(low_ref, group), part, preferred_element_type=jnp.float32)
        inner_ref[:, pl.ds(col, 128)] = total
        return carry

    lax.fori_loop(first_tile, last_tile, body, 0)


def scan_kernel(
    count, parts, ending_ref, decay_ref, high_ref, low_ref, kv_ref, entering_ref, inner_ref, sent, landed, send_sem, recv_sem
):
    me = lax.axis_index("ctx")
    first, later = scan_shifts(count)
    partners = sorted(set(first + later))
    share = ending_ref.shape[1] // parts

    barrier = pltpu.get_barrier_semaphore()
    for span in partners:
        for target in (lax.rem(me + span, count), lax.rem(me + count - span, count)):
            pl.semaphore_signal(barrier, inc=1, device_id={"ctx": target}, device_id_type=pl.DeviceIdType.MESH)
    pl.semaphore_wait(barrier, 2 * len(partners))

    started = []

    def send(source, slot, part, span):
        copy = pltpu.make_async_remote_copy(
            src_ref=source,
            dst_ref=landed.at[slot, part],
            send_sem=send_sem.at[slot, part],
            recv_sem=recv_sem.at[slot, part],
            device_id={"ctx": lax.rem(me + span, count)},
            device_id_type=pl.DeviceIdType.MESH,
        )

        @pl.when(me + span < count)
        def _():
            copy.start()

        started.append((copy, span))
        return (copy, slot, part, span)

    def take(copy, slot, part, span, factor):
        columns = pl.ds(part * share, share)

        @pl.when(me >= span)
        def _():
            copy.wait_recv()
            if factor is None:
                entering_ref[:, columns] += landed[slot, part]
            else:
                entering_ref[:, columns] += decay_ref[factor, :, columns] * landed[slot, part]

    tiles = kv_ref.shape[1] // 128
    rounds = 1 + len(later)
    bounds = [tiles * step // rounds for step in range(rounds + 1)]

    entering_ref[...] = jnp.zeros(entering_ref.shape, jnp.float32)
    pending = []
    for part in range(parts):
        columns = pl.ds(part * share, share)
        pending.append(
            [
                send(ending_ref.at[:, columns], slot, part, span) + (None if slot == 0 else 0,)
                for slot, span in enumerate(first)
            ]
        )
    conv_tiles(high_ref, low_ref, kv_ref, inner_ref, bounds[0], bounds[1])
    for step in range(len(later) + 1):
        for part in range(parts):
            for copy, slot, owner, span, factor in pending[part]:
                take(copy, slot, owner, span, factor)
            if step < len(later):
                slot = len(first) + step
                sent[step, part] = entering_ref[:, pl.ds(part * share, share)]
                pending[part] = [send(sent.at[step, part], slot, part, later[step]) + (step + 1,)]
        if step < len(later):
            conv_tiles(high_ref, low_ref, kv_ref, inner_ref, bounds[step + 1], bounds[step + 2])
    for copy, span in started:

        @pl.when(me + span < count)
        def _():
            copy.wait_send()


def scan_states(ending, decay, high, low, kv, parts=4):
    count = lax.axis_size("ctx")
    first, later = scan_shifts(count)
    slots = len(first) + len(later)
    share = (ending.shape[0], ending.shape[1] // parts)
    vmem = pl.BlockSpec(memory_space=pltpu.VMEM)
    return pl.pallas_call(
        functools.partial(scan_kernel, count, parts),
        out_shape=(
            jax.ShapeDtypeStruct(ending.shape, jnp.float32),
            jax.ShapeDtypeStruct(kv.shape, jnp.float32),
        ),
        in_specs=[vmem] * 5,
        out_specs=(vmem, vmem),
        scratch_shapes=[
            pltpu.VMEM((max(1, len(later)), parts) + share, jnp.float32),
            pltpu.VMEM((slots, parts) + share, jnp.float32),
            pltpu.SemaphoreType.DMA((slots, parts)),
            pltpu.SemaphoreType.DMA((slots, parts)),
        ],
        compiler_params=pltpu.CompilerParams(
            collective_id=0, has_side_effects=True, vmem_limit_bytes=48 * 1024 * 1024
        ),
    )(ending, decay, high, low, kv)


def local(query_in, key_in, value_in, feature_taps, decay_rate, residues, skip_gain, out_weight):
    pair = [(0, 1), (1, 0)]
    chip = lax.axis_index("zlo")
    core = lax.axis_index("core")
    cores = lax.axis_size("core")
    other_chip = (1 - chip) * cores
    remote = lax.ppermute(out_weight, "zlo", pair)
    weight_blocks = [
        (chip * cores + core, out_weight),
        (chip * cores + 1 - core, lax.ppermute(out_weight, "core", pair)),
        (other_chip + core, remote),
    ]
    query_rows = query_in[0]
    key_rows = key_in[0]
    value_rows = value_in[0]
    rows_here, chans = query_rows.shape
    keep = FEAT - 1
    tails = shifted(
        jnp.concatenate(
            [query_rows[rows_here - keep :], key_rows[rows_here - keep :], value_rows[rows_here - keep :]],
            axis=0,
        ),
        "ctx",
        1,
    )
    featured_q = featurize(query_rows, tails[0:keep], feature_taps[0])
    featured_k = featurize(key_rows, tails[keep : 2 * keep], feature_taps[1])
    featured_v = featurize(value_rows, tails[2 * keep :], feature_taps[2])
    kv_round = lax.optimization_barrier((featured_k * featured_v).astype(jnp.bfloat16))

    groups = chans // GROUP
    width = rows_here
    kv_grouped = kv_round.reshape(width, groups, GROUP)

    positions = jnp.arange(width, dtype=jnp.float32)
    scale = residues * jnp.sqrt(-jnp.expm1(-2.0 * decay_rate))
    powers = jnp.exp(-decay_rate[:, :, None] * positions)
    kernel = jnp.einsum("gm,gmt->gt", scale, powers, precision=exact_precision)
    closing = jnp.exp(-decay_rate[:, :, None] * (width - 1.0 - positions))

    taps = jnp.roll(kernel[:, ::-1], 1, axis=1)
    high = lax.reduce_precision(taps, exponent_bits=8, mantissa_bits=7)
    low = lax.reduce_precision(taps - high, exponent_bits=8, mantissa_bits=7)
    ending = two_pass("gnj,jgc->ngc", closing, kv_grouped).reshape(-1, chans)

    first, later = scan_shifts(lax.axis_size("ctx"))
    spans = jnp.asarray([1] * (len(first) - 1) + later, jnp.float32)[:, None, None] * float(width)
    modes = decay_rate.shape[1]
    rate_lanes = jnp.broadcast_to(jnp.transpose(decay_rate)[:, :, None], (modes, groups, GROUP))
    decay = jnp.exp(-rate_lanes.reshape(1, modes, chans) * spans)
    entering, inner = scan_states(ending, decay, high, low, kv_round)
    entering, remote = lax.optimization_barrier((entering, remote))
    weight_blocks.append((other_chip + 1 - core, lax.ppermute(remote, "core", [(0, 1), (1, 0)])))
    scale_lanes = jnp.broadcast_to(jnp.transpose(scale)[:, :, None], (modes, groups, GROUP)).reshape(modes, 1, chans)
    fine_len = 8
    rate_rows = rate_lanes.reshape(modes, 1, 1, chans)
    coarse = jnp.exp(-rate_rows * (fine_len * jnp.arange(width // fine_len, dtype=jnp.float32))[None, :, None, None])
    fine = jnp.exp(-rate_rows * (jnp.arange(fine_len, dtype=jnp.float32) + 1.0)[None, None, :, None])
    weighted = (scale_lanes.reshape(modes, chans) * entering)[:, None, None, :]
    crossing = jnp.sum(weighted * coarse * fine, axis=0).reshape(width, chans)
    convolved = lax.optimization_barrier((inner + crossing).astype(jnp.bfloat16))

    gated = (
        featured_q * (convolved.astype(jnp.float32) + skip_gain * kv_round.astype(jnp.float32))
    ).astype(jnp.bfloat16)
    rows = out_weight.shape[0]
    block_out = None
    for owner, weight in weight_blocks:
        columns = lax.dynamic_slice_in_dim(gated, owner * rows, rows, axis=1)
        term = jnp.dot(columns, weight, preferred_element_type=jnp.float32)
        block_out = term if block_out is None else block_out + term
    return block_out.astype(jnp.bfloat16)[None]


def solution(mesh):
    ctx_size, fsdp_size = mesh.shape["ctx"], mesh.shape["fsdp"]
    split = jax.sharding.Mesh(
        mesh.devices.reshape(ctx_size, fsdp_size // 2, 2), ("ctx", "zlo", "core")
    )
    batch = ("zlo", "core")
    return jax.shard_map(
        local,
        mesh=split,
        in_specs=(
            P(batch, "ctx", None),
            P(batch, "ctx", None),
            P(batch, "ctx", None),
            P(),
            P(),
            P(),
            P(),
            P(batch, None),
        ),
        out_specs=P(batch, "ctx", None),
        check_vma=False,
    )
```

```python
import functools

import jax
import jax.numpy as jnp
from jax import lax
from jax.experimental import pallas as pl
from jax.experimental.pallas import tpu as pltpu
from jax.sharding import PartitionSpec as P

GROUP = 16
FEAT = 3

exact_precision = lax.Precision.HIGHEST


def shifted(shard, axis, by):
    count = lax.axis_size(axis)
    pairs = [(i, i + by) for i in range(count) if 0 <= i + by < count]
    return lax.ppermute(shard, axis, pairs)


def featurize(rows, tail, taps_one):
    values = jnp.concatenate([tail, rows], axis=0).astype(jnp.float32)
    count = rows.shape[0]
    total = taps_one[0] * values[FEAT - 1 :]
    for offset in range(1, FEAT):
        total = total + taps_one[offset] * values[FEAT - 1 - offset : FEAT - 1 - offset + count]
    return total


def split_bf16(values):
    rounded = lax.reduce_precision(values, exponent_bits=8, mantissa_bits=7)
    return rounded.astype(jnp.bfloat16), (values - rounded).astype(jnp.bfloat16)


def two_pass(spec, table, signal):
    high, low = split_bf16(table)
    first = jnp.einsum(spec, high, signal, preferred_element_type=jnp.float32)
    return first + jnp.einsum(spec, low, signal, preferred_element_type=jnp.float32)


def scan_shifts(count):
    first = [1, 2] if count > 2 else [1]
    later = []
    span = 2
    while span < count:
        later.append(span)
        span *= 2
    return first, later


def conv_tiles(high_ref, low_ref, kv_ref, inner_ref, first_tile, last_tile):
    width = kv_ref.shape[0]
    per_tile = 128 // GROUP
    owner = lax.broadcasted_iota(jnp.int32, (1, 128), 1) // GROUP
    causal = lax.broadcasted_iota(jnp.int32, (width, width), 1) <= lax.broadcasted_iota(
        jnp.int32, (width, width), 0
    )

    def toeplitz_part(ref, group):
        row = ref[pl.ds(group, 1), :]
        rolled = pltpu.roll(jnp.broadcast_to(row, (width, width)), 0, 1, stride=1, stride_axis=0)
        return jnp.where(causal, rolled, 0.0).astype(jnp.bfloat16)

    def body(tile, carry):
        col = pl.multiple_of(tile * 128, 128)
        block = kv_ref[:, pl.ds(col, 128)]
        total = jnp.zeros((width, 128), jnp.float32)
        for member in range(per_tile):
            group = tile * per_tile + member
            part = jnp.where(owner == member, block, jnp.zeros_like(block))
            total += jnp.dot(toeplitz_part(high_ref, group), part, preferred_element_type=jnp.float32)
            total += jnp.dot(toeplitz_part(low_ref, group), part, preferred_element_type=jnp.float32)
        inner_ref[:, pl.ds(col, 128)] = total
        return carry

    lax.fori_loop(first_tile, last_tile, body, 0)


def scan_kernel(
    count, parts, ending_ref, decay_ref, high_ref, low_ref, kv_ref, entering_ref, inner_ref, sent, landed, send_sem, recv_sem
):
    me = lax.axis_index("ctx")
    first, later = scan_shifts(count)
    partners = sorted(set(first + later))
    share = ending_ref.shape[1] // parts

    barrier = pltpu.get_barrier_semaphore()
    for span in partners:
        for target in (lax.rem(me + span, count), lax.rem(me + count - span, count)):
            pl.semaphore_signal(barrier, inc=1, device_id={"ctx": target}, device_id_type=pl.DeviceIdType.MESH)
    pl.semaphore_wait(barrier, 2 * len(partners))

    started = []

    def send(source, slot, part, span):
        copy = pltpu.make_async_remote_copy(
            src_ref=source,
            dst_ref=landed.at[slot, part],
            send_sem=send_sem.at[slot, part],
            recv_sem=recv_sem.at[slot, part],
            device_id={"ctx": lax.rem(me + span, count)},
            device_id_type=pl.DeviceIdType.MESH,
        )

        @pl.when(me + span < count)
        def _():
            copy.start()

        started.append((copy, span))
        return (copy, slot, part, span)

    def take(copy, slot, part, span, factor):
        columns = pl.ds(part * share, share)

        @pl.when(me >= span)
        def _():
            copy.wait_recv()
            if factor is None:
                entering_ref[:, columns] += landed[slot, part]
            else:
                entering_ref[:, columns] += decay_ref[factor, :, columns] * landed[slot, part]

    tiles = kv_ref.shape[1] // 128
    rounds = 1 + len(later)
    bounds = [tiles * step // rounds for step in range(rounds + 1)]

    entering_ref[...] = jnp.zeros(entering_ref.shape, jnp.float32)
    pending = []
    for part in range(parts):
        columns = pl.ds(part * share, share)
        pending.append(
            [
                send(ending_ref.at[:, columns], slot, part, span) + (None if slot == 0 else 0,)
                for slot, span in enumerate(first)
            ]
        )
    conv_tiles(high_ref, low_ref, kv_ref, inner_ref, bounds[0], bounds[1])
    for step in range(len(later) + 1):
        for part in range(parts):
            for copy, slot, owner, span, factor in pending[part]:
                take(copy, slot, owner, span, factor)
            if step < len(later):
                slot = len(first) + step
                sent[step, part] = entering_ref[:, pl.ds(part * share, share)]
                pending[part] = [send(sent.at[step, part], slot, part, later[step]) + (step + 1,)]
        if step < len(later):
            conv_tiles(high_ref, low_ref, kv_ref, inner_ref, bounds[step + 1], bounds[step + 2])
    for copy, span in started:

        @pl.when(me + span < count)
        def _():
            copy.wait_send()


def scan_states(ending, decay, high, low, kv, parts=4):
    count = lax.axis_size("ctx")
    first, later = scan_shifts(count)
    slots = len(first) + len(later)
    share = (ending.shape[0], ending.shape[1] // parts)
    vmem = pl.BlockSpec(memory_space=pltpu.VMEM)
    return pl.pallas_call(
        functools.partial(scan_kernel, count, parts),
        out_shape=(
            jax.ShapeDtypeStruct(ending.shape, jnp.float32),
            jax.ShapeDtypeStruct(kv.shape, jnp.float32),
        ),
        in_specs=[vmem] * 5,
        out_specs=(vmem, vmem),
        scratch_shapes=[
            pltpu.VMEM((max(1, len(later)), parts) + share, jnp.float32),
            pltpu.VMEM((slots, parts) + share, jnp.float32),
            pltpu.SemaphoreType.DMA((slots, parts)),
            pltpu.SemaphoreType.DMA((slots, parts)),
        ],
        compiler_params=pltpu.CompilerParams(
            collective_id=0, has_side_effects=True, vmem_limit_bytes=48 * 1024 * 1024
        ),
    )(ending, decay, high, low, kv)


def local(query_in, key_in, value_in, feature_taps, decay_rate, residues, skip_gain, out_weight):
    pair = [(0, 1), (1, 0)]
    chip = lax.axis_index("zlo")
    core = lax.axis_index("core")
    cores = lax.axis_size("core")
    other_chip = (1 - chip) * cores
    remote = lax.ppermute(out_weight, "zlo", pair)
    weight_blocks = [
        (chip * cores + core, out_weight),
        (chip * cores + 1 - core, lax.ppermute(out_weight, "core", pair)),
        (other_chip + core, remote),
    ]
    query_rows = query_in[0]
    key_rows = key_in[0]
    value_rows = value_in[0]
    rows_here, chans = query_rows.shape
    keep = FEAT - 1
    tails = shifted(
        jnp.concatenate(
            [query_rows[rows_here - keep :], key_rows[rows_here - keep :], value_rows[rows_here - keep :]],
            axis=0,
        ),
        "ctx",
        1,
    )
    featured_q = featurize(query_rows, tails[0:keep], feature_taps[0])
    featured_k = featurize(key_rows, tails[keep : 2 * keep], feature_taps[1])
    featured_v = featurize(value_rows, tails[2 * keep :], feature_taps[2])
    kv_round = lax.optimization_barrier((featured_k * featured_v).astype(jnp.bfloat16))

    groups = chans // GROUP
    width = rows_here
    kv_grouped = kv_round.reshape(width, groups, GROUP)

    positions = jnp.arange(width, dtype=jnp.float32)
    scale = residues * jnp.sqrt(-jnp.expm1(-2.0 * decay_rate))
    powers = jnp.exp(-decay_rate[:, :, None] * positions)
    kernel = jnp.einsum("gm,gmt->gt", scale, powers, precision=exact_precision)

    taps = jnp.roll(kernel[:, ::-1], 1, axis=1)
    high = lax.reduce_precision(taps, exponent_bits=8, mantissa_bits=7)
    low = lax.reduce_precision(taps - high, exponent_bits=8, mantissa_bits=7)
    modes = decay_rate.shape[1]
    rate_lanes = jnp.broadcast_to(jnp.transpose(decay_rate)[:, :, None], (modes, groups, GROUP))
    fine_len = 8
    rate_rows = rate_lanes.reshape(modes, 1, 1, chans)

    late = jnp.exp(
        -rate_rows * (fine_len * (width // fine_len - 1 - jnp.arange(width // fine_len, dtype=jnp.float32)))[None, :, None, None]
    )
    near = jnp.exp(-rate_rows * (fine_len - 1.0 - jnp.arange(fine_len, dtype=jnp.float32))[None, None, :, None])
    kv_rows = kv_round.astype(jnp.float32).reshape(1, width // fine_len, fine_len, chans)
    ending = jnp.sum(late * near * kv_rows, axis=(1, 2))

    first, later = scan_shifts(lax.axis_size("ctx"))
    spans = jnp.asarray([1] * (len(first) - 1) + later, jnp.float32)[:, None, None] * float(width)
    decay = jnp.exp(-rate_lanes.reshape(1, modes, chans) * spans)
    entering, inner = scan_states(ending, decay, high, low, kv_round)
    entering, remote = lax.optimization_barrier((entering, remote))
    weight_blocks.append((other_chip + 1 - core, lax.ppermute(remote, "core", [(0, 1), (1, 0)])))
    scale_lanes = jnp.broadcast_to(jnp.transpose(scale)[:, :, None], (modes, groups, GROUP)).reshape(modes, 1, chans)
    coarse = jnp.exp(-rate_rows * (fine_len * jnp.arange(width // fine_len, dtype=jnp.float32))[None, :, None, None])
    fine = jnp.exp(-rate_rows * (jnp.arange(fine_len, dtype=jnp.float32) + 1.0)[None, None, :, None])
    weighted = (scale_lanes.reshape(modes, chans) * entering)[:, None, None, :]
    crossing = jnp.sum(weighted * coarse * fine, axis=0).reshape(width, chans)
    convolved = lax.optimization_barrier((inner + crossing).astype(jnp.bfloat16))

    gated = (
        featured_q * (convolved.astype(jnp.float32) + skip_gain * kv_round.astype(jnp.float32))
    ).astype(jnp.bfloat16)
    rows = out_weight.shape[0]
    block_out = None
    for owner, weight in weight_blocks:
        columns = lax.dynamic_slice_in_dim(gated, owner * rows, rows, axis=1)
        term = jnp.dot(columns, weight, preferred_element_type=jnp.float32)
        block_out = term if block_out is None else block_out + term
    return block_out.astype(jnp.bfloat16)[None]


def solution(mesh):
    ctx_size, fsdp_size = mesh.shape["ctx"], mesh.shape["fsdp"]
    split = jax.sharding.Mesh(
        mesh.devices.reshape(ctx_size, fsdp_size // 2, 2), ("ctx", "zlo", "core")
    )
    batch = ("zlo", "core")
    return jax.shard_map(
        local,
        mesh=split,
        in_specs=(
            P(batch, "ctx", None),
            P(batch, "ctx", None),
            P(batch, "ctx", None),
            P(),
            P(),
            P(),
            P(),
            P(batch, None),
        ),
        out_specs=P(batch, "ctx", None),
        check_vma=False,
    )
```
